512 devices in a mesh: rows: 128 (over y, z, core), rep: 4 (over x).
Axes of the slice: x: 4, y: 8, z: 8, core: 2. Of those that a mesh axis runs over, the one named last changes fastest.
Arguments:
- pivots: int32 [2, 256], replicated, may hold values from 0 to 61439, as said below
- previous: float32 [61440, 1536], P('rows', 'rep'), may hold values from -0.3 to 0.3
- columns: float32 [61440, 512], P(('rows', 'rep')), may hold values from -16 to 16
- diagonal: float32 [61440], P(('rows', 'rep')), may hold values from 2 to 6
Outputs:
- vectors: float32 [61440, 512], P(('rows', 'rep'))
- diag_out: float32 [61440], P(('rows', 'rep'))
The draws below stay inside these ranges and needn't reach their ends.
Inputs may be any that keep to these rules, and one draw needn't show every extreme that they name: 512 different AO-pair indices; the residual blocks at each panel's pivots are positive definite.
All inputs are finite; a program needn't handle non-finite values.
Results may differ from the reference program's by a relative error of at most 0.00011.
Values sent between devices are 32-bit elements; how exact they have to be, the bound alone decides.
A program may use at most 64 MiB of HBM per device.

```python
import jax
import jax.numpy as jnp
from jax import lax

ROWS_DEV = 480
EARLIER = 1536
PANEL = 256
NPAIRS = 61440


highest = lax.Precision.HIGHEST


def build_pivots(key):
    order = jax.random.permutation(jax.random.fold_in(key, 11), NPAIRS).astype(jnp.int32)
    ranks = jnp.zeros((NPAIRS,), jnp.int32).at[order].set(jnp.arange(NPAIRS, dtype=jnp.int32))
    hot_blocks = jax.random.permutation(jax.random.fold_in(key, 12), NPAIRS // ROWS_DEV)[:4].astype(jnp.int32)
    owners = jnp.arange(NPAIRS, dtype=jnp.int32) // ROWS_DEV
    is_hot = jnp.any(owners[:, None] == hot_blocks[None, :], axis=1)
    scores = jnp.where(is_hot, 2 * ranks + 1, 8 * ranks)
    picked = jnp.argsort(scores, stable=True)[:2 * PANEL].astype(jnp.int32)
    return picked.reshape(2, PANEL)


def build_previous(key):
    inner = jax.random.fold_in(key, 21)
    values = jnp.clip(0.05 * jax.random.normal(inner, (NPAIRS, EARLIER), jnp.float32), -0.3, 0.3)
    return values


def gram_block(key):
    factor = jax.random.normal(key, (PANEL, 2 * PANEL), jnp.float32)
    return jnp.dot(factor, factor.T, precision=highest) / (2.0 * PANEL) + 0.5 * jnp.eye(PANEL, dtype=jnp.float32)


def build_columns(key):
    pivots = build_pivots(key)
    previous = build_previous(key)
    inner = jax.random.fold_in(key, 31)
    noise = jnp.clip(0.0625 * jax.random.normal(inner, (NPAIRS, 2 * PANEL), jnp.float32), -0.5, 0.5)
    first_rows = jnp.take(previous, pivots[0], axis=0)
    second_rows = jnp.take(previous, pivots[1], axis=0)
    block_one = gram_block(jax.random.fold_in(key, 33))
    block_two = gram_block(jax.random.fold_in(key, 34))
    top_block = jnp.dot(first_rows, first_rows.T, precision=highest) + block_one
    cross_resid = noise[pivots[1], :PANEL] - jnp.dot(second_rows, first_rows.T, precision=highest)
    factor_one = jnp.linalg.cholesky(block_one)
    cross_rows = jax.scipy.linalg.solve_triangular(factor_one, cross_resid.T, lower=True).T
    bottom_block = jnp.dot(second_rows, second_rows.T, precision=highest) + jnp.dot(cross_rows, cross_rows.T, precision=highest) + block_two
    filled = noise.at[pivots[0], :PANEL].set(top_block)
    filled = filled.at[pivots[1], PANEL:].set(bottom_block)
    return filled


def draw_pivots(key, part):
    return build_pivots(key)


def draw_previous(key, part):
    return build_previous(key)


def draw_columns(key, part):
    return build_columns(key)


def levels(own_key, shape, pieces, smallest, high):
    def one(dim, parts):
        draws = jax.random.uniform(jax.random.fold_in(jax.random.fold_in(own_key, 6), dim), (parts,), jnp.float32, smallest / len(pieces), high / len(pieces))
        return jnp.repeat(jnp.exp(draws), shape[dim] // parts).reshape((-1,) + (1,) * (len(shape) - dim - 1))

    loudness = one(*pieces[0])
    for cut in pieces[1:]:
        loudness = loudness * one(*cut)
    return loudness


def setup_inputs(seed: int = 0) -> dict:
    splits = jax.random.split(jax.random.key(seed), 5)
    pivots = draw_pivots(jax.random.fold_in(splits[4], 71), 0)
    previous = draw_previous(jax.random.fold_in(splits[4], 71), 0)
    columns = draw_columns(jax.random.fold_in(splits[4], 71), 0)
    diagonal = jnp.clip(2.0 + 4.0 * jax.random.uniform(splits[3], (NPAIRS,), jnp.float32) ** levels(splits[3], (NPAIRS,), ((0, 512),), -0.2, 0.2), 2.0, 6.0)
    return dict(pivots=pivots, previous=previous, columns=columns, diagonal=diagonal)


highest = lax.Precision.HIGHEST

def reference(pivots, previous, columns, diagonal):
    all_pivots = pivots.reshape(-1).astype(jnp.int32)
    chosen = jnp.take(previous, all_pivots, axis=0)
    resid = columns - lax.dot_general(previous.astype(jnp.float32), chosen.astype(jnp.float32), (((1,), (1,)), ((), ())), precision=highest, preferred_element_type=jnp.float32)
    first_part = resid[:, :PANEL]
    factor_one = jnp.linalg.cholesky(jnp.take(first_part, pivots[0], axis=0))
    vec_one = jax.scipy.linalg.solve_triangular(factor_one, first_part.T, lower=True).T
    cross_rows = jnp.take(vec_one, pivots[1], axis=0)
    rest = resid[:, PANEL:] - lax.dot_general(vec_one.astype(jnp.float32), cross_rows.astype(jnp.float32), (((1,), (1,)), ((), ())), precision=highest, preferred_element_type=jnp.float32)
    factor_two = jnp.linalg.cholesky(jnp.take(rest, pivots[1], axis=0))
    vec_two = jax.scipy.linalg.solve_triangular(factor_two, rest.T, lower=True).T
    vectors = jnp.concatenate([vec_one, vec_two], axis=1)
    diag_out = diagonal - jnp.sum(vec_one * vec_one, axis=1) - jnp.sum(vec_two * vec_two, axis=1)
    return (vectors, diag_out)
```

```python
import functools

import jax
import jax.numpy as jnp
from jax import lax
from jax.experimental import pallas as pl
from jax.experimental.pallas import tpu as pltpu
from jax.sharding import PartitionSpec as P

HIGHEST = lax.Precision.HIGHEST
MESH = pl.DeviceIdType.MESH
PANEL = 256
EARLY = 384
SIDE = 8
REPS = 4
CHUNK = PANEL // 2 // SIDE
WIDTHS = (EARLY + PANEL, EARLY + 2 * PANEL)


def dot_nt(left, right, precision=HIGHEST):
    return lax.dot_general(
        left, right, (((1,), (1,)), ((), ())), precision=precision, preferred_element_type=jnp.float32
    )


def pick(mask, values):
    total = None
    for _ in range(3):
        part = values.astype(jnp.bfloat16)
        values = values - part.astype(jnp.float32)
        term = lax.dot_general(
            mask, part, (((0,), (0,)), ((), ())), preferred_element_type=jnp.float32
        )
        total = term if total is None else total + term
    return total


def kernel(
    pivots_ref, previous_ref, columns_ref,
    g11_ref, g21_ref, g22_ref, resid_ref,
    pick0, pick1, pair0, pair1, half0, half1, first0, first1, own0, own1, second0, second1,
    full0, full1, gpart0, gpart1, gx0, gx1, gsum0, gsum1, partial, rres,
    pair_sems, axis_sems, fwd_sems, gx_sems, gpair_sems, res_sems,
):
    rows = lax.axis_index("rows")
    rep = lax.axis_index("rep")
    core = lax.rem(rows, 2)
    chip_z = lax.rem(rows // 2, SIDE)
    chip_y = rows // (2 * SIDE)
    spot = (1 - core) * chip_y + core * chip_z

    def at(y, z, c):
        return (y * SIDE + z) * 2 + c

    def first_peer(d):
        y = lax.rem(chip_y + (1 - core) * d, SIDE)
        z = lax.rem(chip_z + core * d, SIDE)
        return at(y, z, core), lax.rem(spot + d, SIDE)

    def second_peer(d):
        y = lax.rem(chip_y + core * d, SIDE)
        z = lax.rem(chip_z + (1 - core) * d, SIDE)
        return at(y, z, core)

    partner = at(chip_y, chip_z, 1 - core)
    barrier = pltpu.get_barrier_semaphore()
    for d in range(1, SIDE):
        pl.semaphore_signal(barrier, inc=1, device_id=(first_peer(d)[0], rep), device_id_type=MESH)
        pl.semaphore_signal(barrier, inc=1, device_id=(second_peer(d), rep), device_id_type=MESH)
    for d in range(1, REPS):
        pl.semaphore_signal(barrier, inc=1, device_id=(rows, lax.rem(rep + d, REPS)), device_id_type=MESH)
    pl.semaphore_signal(barrier, inc=1, device_id=(partner, rep), device_id_type=MESH)

    def send(src, dst, sems, slot, where):
        copy = pltpu.make_async_remote_copy(
            src_ref=src, dst_ref=dst, send_sem=sems.at[(0,) + slot], recv_sem=sems.at[(1,) + slot],
            device_id=where, device_id_type=MESH,
        )
        copy.start()
        return copy

    block_rows = previous_ref.shape[0]
    own_rows = columns_ref.shape[0]
    picks, pairs, halves, firsts = (pick0, pick1), (pair0, pair1), (half0, half1), (first0, first1)
    owns, seconds, fulls = (own0, own1), (second0, second1), (full0, full1)
    gparts, gxs, gsums = (gpart0, gpart1), (gx0, gx1), (gsum0, gsum1)

    def make_picks(p):
        index = pivots_ref[p:p + 1, :]
        block = lax.broadcasted_iota(jnp.int32, (block_rows, PANEL), 0) + rows * block_rows
        mask = jnp.where(block == index, 1.0, 0.0).astype(jnp.bfloat16)
        picks[p][:, :EARLY] = pick(mask, previous_ref[...])
        own = lax.broadcasted_iota(jnp.int32, (own_rows, PANEL), 0) + (rows * REPS + rep) * own_rows
        mask = jnp.where(own == index, 1.0, 0.0)
        values = columns_ref[:, :WIDTHS[p] - EARLY]
        pad = jnp.zeros((-own_rows % 16, PANEL), jnp.float32)
        mask = jnp.concatenate([mask, pad], axis=0).astype(jnp.bfloat16)
        pad = jnp.zeros((-own_rows % 16, values.shape[1]), jnp.float32)
        picks[p][:, EARLY:] = pick(mask, jnp.concatenate([values, pad], axis=0))

    def start_pair(p):
        src = picks[p].at[pl.ds((1 - core) * (PANEL // 2), PANEL // 2), :]
        return send(src, pairs[p], pair_sems, (p,), (partner, rep))

    def start_first(p, pair_copy):
        pair_copy.wait()
        halves[p][...] = picks[p][pl.ds(core * (PANEL // 2), PANEL // 2), :] + pairs[p][...]
        copies = []
        for d in (4, 3, 5, 2, 6, 1, 7):
            peer, place = first_peer(d)
            src = halves[p].at[pl.ds(place * CHUNK, CHUNK), :]
            copies.append(send(src, firsts[p].at[d - 1], axis_sems, (p, 0, d - 1), (peer, rep)))
        return copies

    def start_second(p, copies):
        total = halves[p][pl.ds(spot * CHUNK, CHUNK), :]
        for copy in copies:
            copy.wait()
        for d in range(1, SIDE):
            total = total + firsts[p][d - 1]
        owns[p][0] = total
        result = []
        for d in (4, 3, 5, 2, 6, 1, 7):
            result.append(send(owns[p].at[0], seconds[p].at[d - 1], axis_sems, (p, 1, d - 1), (second_peer(d), rep)))
        return result

    def start_gather(p, copies):
        for copy in copies:
            copy.wait()
        total = owns[p][0]
        for d in range(1, SIDE):
            total = total + seconds[p][d - 1]
        owns[p][1] = total
        place = pl.ds(core * (PANEL // 2) + spot * CHUNK, CHUNK)
        fulls[p][place, :] = total
        result = []
        for d in (4, 3, 5, 2, 6, 1, 7):
            peer, _ = first_peer(d)
            result.append(send(owns[p].at[1], fulls[p].at[place, :], axis_sems, (p, 2, d - 1), (peer, rep)))
        result.append(send(owns[p].at[1], fulls[p].at[place, :], fwd_sems, (p, 0), (partner, rep)))
        return result

    def finish_gather(p, copies):
        forwards = []
        order = (4, 3, 5, 2, 6, 1, 7)
        for i in (5, 6, 3, 4, 1, 2, 0):
            d = order[i]
            copies[i].wait()
            source = lax.rem(spot + SIDE - d, SIDE)
            place = pl.ds(core * (PANEL // 2) + source * CHUNK, CHUNK)
            forwards.append(send(fulls[p].at[place, :], fulls[p].at[place, :], fwd_sems, (p, d), (partner, rep)))
        copies[7].wait()
        for copy in forwards:
            copy.wait()

    def start_gsum(p):
        chosen = fulls[p][:, :EARLY]
        cols = fulls[p][:, EARLY:]
        b = PANEL // 2
        if p == 0:
            g = cols - dot_nt(chosen, chosen)
        else:
            g = cols[:, PANEL:] - dot_nt(chosen, chosen)
            g21 = cols[:, :PANEL] - dot_nt(chosen, fulls[0][:, :EARLY])
            gparts[p][3 * b:5 * b] = g21[:, :b]
            gparts[p][5 * b:7 * b] = g21[:, b:]
        gparts[p][0:b] = g[:b, :b]
        gparts[p][b:2 * b] = 0.5 * (g[b:, :b] + g[:b, b:].T)
        gparts[p][2 * b:3 * b] = g[b:, b:]
        size = gparts[p].shape[0] // 2
        mine = pl.ds(core * size, size)
        copies = []
        for d in (2, 1, 3):
            where = (rows, lax.rem(rep + d, REPS))
            copies.append(send(gparts[p].at[mine, :], gxs[p].at[d - 1], gx_sems, (p, d - 1), where))
        return copies

    def start_gpair(p, copies):
        size = gparts[p].shape[0] // 2
        mine = pl.ds(core * size, size)
        for copy in copies:
            copy.wait()
        gsums[p][mine, :] = gparts[p][mine, :] + gxs[p][0] + gxs[p][1] + gxs[p][2]
        return send(gsums[p].at[mine, :], gsums[p].at[mine, :], gpair_sems, (p,), (partner, rep))

    def symmetric(p):
        b = PANEL // 2
        g = gsums[p]
        one, mid, two = g[0:b], g[b:2 * b], g[2 * b:3 * b]
        return 0.5 * (one + one.T), mid, 0.5 * (two + two.T)

    def store_square(ref, parts):
        b = PANEL // 2
        one, mid, two = parts
        ref[:b, :b] = one
        ref[b:, :b] = mid
        ref[:b, b:] = mid.T
        ref[b:, b:] = two

    def start_resid():
        for p in range(2):
            partial[:, p * PANEL:(p + 1) * PANEL] = dot_nt(previous_ref[...], fulls[p][:, :EARLY])
        copies = []
        for d in (2, 1, 3):
            other = lax.rem(rep + d, REPS)
            src = partial.at[pl.ds(other * own_rows, own_rows), :]
            copies.append(send(src, rres.at[d - 1], res_sems, (d - 1,), (rows, other)))
        return copies

    def finish_resid(copies):
        for copy in copies:
            copy.wait()
        mine = partial[pl.ds(rep * own_rows, own_rows), :]
        resid_ref[...] = columns_ref[...] - (((mine + rres[0]) + rres[1]) + rres[2])

    make_picks(0)
    pl.semaphore_wait(barrier, 2 * (SIDE - 1) + REPS)
    pair_a = start_pair(0)
    make_picks(1)
    first_a = start_first(0, pair_a)
    pair_b = start_pair(1)
    second_a = start_second(0, first_a)
    first_b = start_first(1, pair_b)
    gather_a = start_gather(0, second_a)
    second_b = start_second(1, first_b)
    finish_gather(0, gather_a)
    gx_a = start_gsum(0)
    gather_b = start_gather(1, second_b)
    gpair_a = start_gpair(0, gx_a)
    finish_gather(1, gather_b)
    gx_b = start_gsum(1)
    res = start_resid()
    gpair_a.wait()
    store_square(g11_ref, symmetric(0))
    gpair_b = start_gpair(1, gx_b)
    gpair_b.wait()
    b = PANEL // 2
    store_square(g22_ref, symmetric(1))
    g21_ref[:, :b] = gsum1[3 * b:5 * b]
    g21_ref[:, b:] = gsum1[5 * b:7 * b]
    finish_resid(res)


def solve_right(factor, matrix):
    return jax.scipy.linalg.solve_triangular(factor, matrix.T, lower=True).T


def communicate(pivots, previous, columns):
    f32 = jnp.float32
    own_rows = columns.shape[0]
    vmem = lambda *shape: pltpu.VMEM(shape, f32)
    two = lambda build: [build(WIDTHS[0]), build(WIDTHS[1])]
    scratch = []
    scratch += two(lambda w: vmem(PANEL, w))
    scratch += two(lambda w: vmem(PANEL // 2, w))
    scratch += two(lambda w: vmem(PANEL // 2, w))
    scratch += two(lambda w: vmem(SIDE - 1, CHUNK, w))
    scratch += two(lambda w: vmem(2, CHUNK, w))
    scratch += two(lambda w: vmem(SIDE - 1, CHUNK, w))
    scratch += two(lambda w: vmem(PANEL, w))
    scratch += [vmem(384, 128), vmem(896, 128)]
    scratch += [vmem(REPS - 1, 192, 128), vmem(REPS - 1, 448, 128)]
    scratch += [vmem(384, 128), vmem(896, 128)]
    scratch += [vmem(previous.shape[0], 2 * PANEL), vmem(REPS - 1, own_rows, 2 * PANEL)]
    dma = pltpu.SemaphoreType.DMA
    scratch += [
        dma((2, 2)), dma((2, 2, 3, SIDE - 1)), dma((2, 2, SIDE)),
        dma((2, 2, REPS - 1)), dma((2, 2)), dma((2, REPS - 1)),
    ]
    square = jax.ShapeDtypeStruct((PANEL, PANEL), f32)
    return pl.pallas_call(
        kernel,
        out_shape=(square, square, square, jax.ShapeDtypeStruct(columns.shape, f32)),
        in_specs=[pl.BlockSpec(memory_space=pltpu.VMEM)] * 3,
        out_specs=[pl.BlockSpec(memory_space=pltpu.VMEM)] * 4,
        scratch_shapes=scratch,
        compiler_params=pltpu.CompilerParams(collective_id=0, has_side_effects=True),
    )(pivots, previous, columns)


def per_device(pivots, previous, columns, diagonal):
    g11, g21, g22, resid = communicate(pivots, previous, columns)
    first_part, second_part = resid[:, :PANEL], resid[:, PANEL:]
    factor_one = jnp.linalg.cholesky(g11)
    solved = solve_right(factor_one, jnp.concatenate([first_part, g21], axis=0))
    vec_one, cross_rows = solved[:first_part.shape[0]], solved[first_part.shape[0]:]
    factor_two = jnp.linalg.cholesky(g22 - dot_nt(cross_rows, cross_rows))
    rest = second_part - dot_nt(vec_one, cross_rows)
    vec_two = solve_right(factor_two, rest)
    vectors = jnp.concatenate([vec_one, vec_two], axis=1)
    diag_out = diagonal - jnp.sum(vec_one * vec_one, axis=1) - jnp.sum(vec_two * vec_two, axis=1)
    return (vectors, diag_out)


def solution(mesh):
    placed = (P(), P("rows", "rep"), P(("rows", "rep"), None), P(("rows", "rep")))
    return jax.shard_map(
        per_device,
        mesh=mesh,
        in_specs=placed,
        out_specs=(P(("rows", "rep"), None), P(("rows", "rep"))),
        check_vma=False,
    )
```

```python
import functools

import jax
import jax.numpy as jnp
from jax import lax
from jax.experimental import pallas as pl
from jax.experimental.pallas import tpu as pltpu
from jax.sharding import PartitionSpec as P

HIGHEST = lax.Precision.HIGHEST
MESH = pl.DeviceIdType.MESH
PANEL = 256
EARLY = 384
SIDE = 8
REPS = 4
CHUNK = PANEL // 2 // SIDE
WIDTHS = (EARLY + PANEL, EARLY + 2 * PANEL)


def dot_nt(left, right, precision=HIGHEST):
    return lax.dot_general(
        left, right, (((1,), (1,)), ((), ())), precision=precision, preferred_element_type=jnp.float32
    )


def pick(mask, values):
    total = None
    for _ in range(3):
        part = values.astype(jnp.bfloat16)
        values = values - part.astype(jnp.float32)
        term = lax.dot_general(
            mask, part, (((0,), (0,)), ((), ())), preferred_element_type=jnp.float32
        )
        total = term if total is None else total + term
    return total


def kernel(
    pivots_ref, previous_ref, columns_ref,
    g11_ref, g21_ref, g22_ref, resid_ref,
    pick0, pick1, pair0, pair1, half0, half1, first0, first1, own0, own1, second0, second1,
    full0, full1, gpart0, gpart1, gx0, gx1, gsum0, gsum1, partial, rres,
    pair_sems, axis_sems, fwd_sems, gx_sems, gpair_sems, res_sems,
):
    rows = lax.axis_index("rows")
    rep = lax.axis_index("rep")
    core = lax.rem(rows, 2)
    chip_z = lax.rem(rows // 2, SIDE)
    chip_y = rows // (2 * SIDE)
    spot = (1 - core) * chip_y + core * chip_z

    def at(y, z, c):
        return (y * SIDE + z) * 2 + c

    def first_peer(d):
        y = lax.rem(chip_y + (1 - core) * d, SIDE)
        z = lax.rem(chip_z + core * d, SIDE)
        return at(y, z, core), lax.rem(spot + d, SIDE)

    def second_peer(d):
        y = lax.rem(chip_y + core * d, SIDE)
        z = lax.rem(chip_z + (1 - core) * d, SIDE)
        return at(y, z, core)

    partner = at(chip_y, chip_z, 1 - core)
    barrier = pltpu.get_barrier_semaphore()
    for d in range(1, SIDE):
        pl.semaphore_signal(barrier, inc=1, device_id=(first_peer(d)[0], rep), device_id_type=MESH)
        pl.semaphore_signal(barrier, inc=1, device_id=(second_peer(d), rep), device_id_type=MESH)
    for d in range(1, REPS):
        pl.semaphore_signal(barrier, inc=1, device_id=(rows, lax.rem(rep + d, REPS)), device_id_type=MESH)
    pl.semaphore_signal(barrier, inc=1, device_id=(partner, rep), device_id_type=MESH)

    def send(src, dst, sems, slot, where):
        copy = pltpu.make_async_remote_copy(
            src_ref=src, dst_ref=dst, send_sem=sems.at[(0,) + slot], recv_sem=sems.at[(1,) + slot],
            device_id=where, device_id_type=MESH,
        )
        copy.start()
        return copy

    block_rows = previous_ref.shape[0]
    own_rows = columns_ref.shape[0]
    picks, pairs, halves, firsts = (pick0, pick1), (pair0, pair1), (half0, half1), (first0, first1)
    owns, seconds, fulls = (own0, own1), (second0, second1), (full0, full1)
    gparts, gxs, gsums = (gpart0, gpart1), (gx0, gx1), (gsum0, gsum1)

    def make_picks(p):
        index = pivots_ref[p:p + 1, :]
        block = lax.broadcasted_iota(jnp.int32, (block_rows, PANEL), 0) + rows * block_rows
        mask = jnp.where(block == index, 1.0, 0.0).astype(jnp.bfloat16)
        picks[p][:, :EARLY] = pick(mask, previous_ref[...])
        own = lax.broadcasted_iota(jnp.int32, (own_rows, PANEL), 0) + (rows * REPS + rep) * own_rows
        mask = jnp.where(own == index, 1.0, 0.0)
        values = columns_ref[:, :WIDTHS[p] - EARLY]
        pad = jnp.zeros((-own_rows % 16, PANEL), jnp.float32)
        mask = jnp.concatenate([mask, pad], axis=0).astype(jnp.bfloat16)
        pad = jnp.zeros((-own_rows % 16, values.shape[1]), jnp.float32)
        picks[p][:, EARLY:] = pick(mask, jnp.concatenate([values, pad], axis=0))

    def start_pair(p):
        src = picks[p].at[pl.ds((1 - core) * (PANEL // 2), PANEL // 2), :]
        return send(src, pairs[p], pair_sems, (p,), (partner, rep))

    def start_first(p, pair_copy):
        pair_copy.wait()
        halves[p][...] = picks[p][pl.ds(core * (PANEL // 2), PANEL // 2), :] + pairs[p][...]
        copies = []
        for d in (4, 3, 5, 2, 6, 1, 7):
            peer, place = first_peer(d)
            src = halves[p].at[pl.ds(place * CHUNK, CHUNK), :]
            copies.append(send(src, firsts[p].at[d - 1], axis_sems, (p, 0, d - 1), (peer, rep)))
        return copies

    def start_second(p, copies):
        total = halves[p][pl.ds(spot * CHUNK, CHUNK), :]
        for copy in copies:
            copy.wait()
        for d in range(1, SIDE):
            total = total + firsts[p][d - 1]
        owns[p][0] = total
        result = []
        for d in (4, 3, 5, 2, 6, 1, 7):
            result.append(send(owns[p].at[0], seconds[p].at[d - 1], axis_sems, (p, 1, d - 1), (second_peer(d), rep)))
        return result

    def start_gather(p, copies):
        for copy in copies:
            copy.wait()
        total = owns[p][0]
        for d in range(1, SIDE):
            total = total + seconds[p][d - 1]
        owns[p][1] = total
        place = pl.ds(core * (PANEL // 2) + spot * CHUNK, CHUNK)
        fulls[p][place, :] = total
        result = []
        for d in (4, 3, 5, 2, 6, 1, 7):
            peer, _ = first_peer(d)
            result.append(send(owns[p].at[1], fulls[p].at[place, :], axis_sems, (p, 2, d - 1), (peer, rep)))
        result.append(send(owns[p].at[1], fulls[p].at[place, :], fwd_sems, (p, 0), (partner, rep)))
        return result

    def finish_gather(p, copies):
        forwards = []
        order = (4, 3, 5, 2, 6, 1, 7)
        for i in (5, 6, 3, 4, 1, 2, 0):
            d = order[i]
            copies[i].wait()
            source = lax.rem(spot + SIDE - d, SIDE)
            place = pl.ds(core * (PANEL // 2) + source * CHUNK, CHUNK)
            forwards.append(send(fulls[p].at[place, :], fulls[p].at[place, :], fwd_sems, (p, d), (partner, rep)))
        copies[7].wait()
        for copy in forwards:
            copy.wait()

    def start_gsum(p):
        chosen = fulls[p][:, :EARLY]
        cols = fulls[p][:, EARLY:]
        b = PANEL // 2
        if p == 0:
            g = cols - dot_nt(chosen, chosen)
        else:
            g = cols[:, PANEL:] - dot_nt(chosen, chosen)
            g21 = cols[:, :PANEL] - dot_nt(chosen, fulls[0][:, :EARLY])
            gparts[p][3 * b:5 * b] = g21[:, :b]
            gparts[p][5 * b:7 * b] = g21[:, b:]
        gparts[p][0:b] = g[:b, :b]
        gparts[p][b:2 * b] = 0.5 * (g[b:, :b] + g[:b, b:].T)
        gparts[p][2 * b:3 * b] = g[b:, b:]
        size = gparts[p].shape[0] // 2
        mine = pl.ds(core * size, size)
        copies = []
        for d in (2, 1, 3):
            where = (rows, lax.rem(rep + d, REPS))
            copies.append(send(gparts[p].at[mine, :], gxs[p].at[d - 1], gx_sems, (p, d - 1), where))
        return copies

    def start_gpair(p, copies):
        size = gparts[p].shape[0] // 2
        mine = pl.ds(core * size, size)
        for copy in copies:
            copy.wait()
        gsums[p][mine, :] = gparts[p][mine, :] + gxs[p][0] + gxs[p][1] + gxs[p][2]
        return send(gsums[p].at[mine, :], gsums[p].at[mine, :], gpair_sems, (p,), (partner, rep))

    def symmetric(p):
        b = PANEL // 2
        g = gsums[p]
        one, mid, two = g[0:b], g[b:2 * b], g[2 * b:3 * b]
        return 0.5 * (one + one.T), mid, 0.5 * (two + two.T)

    def store_square(ref, parts):
        b = PANEL // 2
        one, mid, two = parts
        ref[:b, :b] = one
        ref[b:, :b] = mid
        ref[:b, b:] = mid.T
        ref[b:, b:] = two

    def start_resid():
        for p in range(2):
            partial[:, p * PANEL:(p + 1) * PANEL] = dot_nt(previous_ref[...], fulls[p][:, :EARLY])
        copies = []
        for d in (2, 1, 3):
            other = lax.rem(rep + d, REPS)
            src = partial.at[pl.ds(other * own_rows, own_rows), :]
            copies.append(send(src, rres.at[d - 1], res_sems, (d - 1,), (rows, other)))
        return copies

    def finish_resid(copies):
        for copy in copies:
            copy.wait()
        mine = partial[pl.ds(rep * own_rows, own_rows), :]
        resid_ref[...] = columns_ref[...] - (((mine + rres[0]) + rres[1]) + rres[2])

    make_picks(0)
    pl.semaphore_wait(barrier, 2 * (SIDE - 1) + REPS)
    pair_a = start_pair(0)
    make_picks(1)
    first_a = start_first(0, pair_a)
    pair_b = start_pair(1)
    second_a = start_second(0, first_a)
    first_b = start_first(1, pair_b)
    gather_a = start_gather(0, second_a)
    second_b = start_second(1, first_b)
    finish_gather(0, gather_a)
    gx_a = start_gsum(0)
    gather_b = start_gather(1, second_b)
    gpair_a = start_gpair(0, gx_a)
    finish_gather(1, gather_b)
    gx_b = start_gsum(1)
    res = start_resid()
    gpair_a.wait()
    store_square(g11_ref, symmetric(0))
    gpair_b = start_gpair(1, gx_b)
    gpair_b.wait()
    b = PANEL // 2
    store_square(g22_ref, symmetric(1))
    g21_ref[:, :b] = gsum1[3 * b:5 * b]
    g21_ref[:, b:] = gsum1[5 * b:7 * b]
    finish_resid(res)


BASE = 32
TILES = BASE // 8


def dot_tn(left, right):
    return lax.dot_general(
        left, right, (((0,), (0,)), ((), ())), precision=HIGHEST, preferred_element_type=jnp.float32
    )


def spread(tile, row):
    return jnp.broadcast_to(tile[row:row + 1, :], tile.shape)


def eliminate(square, wide):
    sub = lax.broadcasted_iota(jnp.int32, (8, 128), 0)
    cols = []
    for k in range(BASE):
        cols.append([None] * TILES)
        for v in range(k // 8, TILES):
            cols[k][v] = jnp.broadcast_to(square[8 * v:8 * v + 8, k:k + 1], (8, 128))
    lanes = wide.shape[1] // 128
    work = [[wide[8 * v:8 * v + 8, 128 * l:128 * l + 128] for l in range(lanes)] for v in range(TILES)]
    pivots = []
    for j in range(BASE):
        top, row = j // 8, j % 8
        pivot = spread(cols[j][top], row)
        pivots.append(pivot)
        inverse = 1.0 / pivot
        factor = [None] * TILES
        for v in range(top, TILES):
            value = cols[j][v] * inverse
            factor[v] = jnp.where(sub > row, value, 0.0) if v == top else value
        for k in range(j + 1, BASE):
            value = spread(cols[j][k // 8], k % 8)
            for v in range(k // 8, TILES):
                cols[k][v] = cols[k][v] - factor[v] * value
        for l in range(lanes):
            value = spread(work[top][l], row)
            for v in range(top, TILES):
                work[v][l] = work[v][l] - factor[v] * value
    out = []
    for v in range(TILES):
        pivot = pivots[8 * v]
        for s in range(1, 8):
            pivot = jnp.where(sub == s, pivots[8 * v + s], pivot)
        scale = lax.rsqrt(pivot)
        scale = scale * (1.5 - 0.5 * pivot * scale * scale)
        out.append(jnp.concatenate([work[v][l] * scale for l in range(lanes)], axis=1))
    return jnp.concatenate(out, axis=0)


def factor_inverse(block_ref, upper_ref):
    for k in range(PANEL // BASE):
        rows = slice(k * BASE, k * BASE + BASE)
        lane = lax.broadcasted_iota(jnp.int32, (BASE, PANEL), 1)
        sub = lax.broadcasted_iota(jnp.int32, (BASE, PANEL), 0)
        wide = jnp.concatenate([block_ref[rows, :], jnp.where(lane == sub + k * BASE, 1.0, 0.0)], axis=1)
        for done in (slice(0, (k - 1) * BASE), slice(max(k - 1, 0) * BASE, k * BASE)):
            if done.stop > done.start:
                wide = wide - dot_tn(upper_ref[done, rows], upper_ref[done, :])
        upper_ref[rows, :] = eliminate(wide[:, rows], wide)


def factor_kernel(g11_ref, g21_ref, g22_ref, resid_ref, diagonal_ref, vectors_ref, diag_ref, upper, cross, block):
    factor_inverse(g11_ref, upper)
    inverse = upper[:, PANEL:]
    cross[...] = dot_nt(g21_ref[...], inverse)
    block[...] = g22_ref[...] - dot_nt(cross[...], cross[...])
    vec_one = dot_nt(resid_ref[:, :PANEL], inverse)
    vectors_ref[:, :PANEL] = vec_one
    vectors_ref[:, PANEL:] = resid_ref[:, PANEL:] - dot_nt(vec_one, cross[...])
    factor_inverse(block, upper)
    vec_two = dot_nt(vectors_ref[:, PANEL:], upper[:, PANEL:])
    vectors_ref[:, PANEL:] = vec_two
    ones = jnp.ones((8, PANEL), jnp.float32)
    sums = dot_nt(ones, vec_one * vec_one) + dot_nt(ones, vec_two * vec_two)
    diag_ref[...] = diagonal_ref[...] - sums[0:1, :]


def factorise(g11, g21, g22, resid, diagonal):
    f32 = jnp.float32
    count = resid.shape[0]
    vmem = pl.BlockSpec(memory_space=pltpu.VMEM)
    vectors, diag = pl.pallas_call(
        factor_kernel,
        out_shape=(jax.ShapeDtypeStruct(resid.shape, f32), jax.ShapeDtypeStruct((1, count), f32)),
        in_specs=[vmem] * 5,
        out_specs=[vmem] * 2,
        scratch_shapes=[
            pltpu.VMEM((PANEL, 2 * PANEL), f32), pltpu.VMEM((PANEL, PANEL), f32), pltpu.VMEM((PANEL, PANEL), f32),
        ],
    )(g11, g21, g22, resid, diagonal.reshape(1, count))
    return vectors, diag.reshape(count)


def communicate(pivots, previous, columns):
    f32 = jnp.float32
    own_rows = columns.shape[0]
    vmem = lambda *shape: pltpu.VMEM(shape, f32)
    two = lambda build: [build(WIDTHS[0]), build(WIDTHS[1])]
    scratch = []
    scratch += two(lambda w: vmem(PANEL, w))
    scratch += two(lambda w: vmem(PANEL // 2, w))
    scratch += two(lambda w: vmem(PANEL // 2, w))
    scratch += two(lambda w: vmem(SIDE - 1, CHUNK, w))
    scratch += two(lambda w: vmem(2, CHUNK, w))
    scratch += two(lambda w: vmem(SIDE - 1, CHUNK, w))
    scratch += two(lambda w: vmem(PANEL, w))
    scratch += [vmem(384, 128), vmem(896, 128)]
    scratch += [vmem(REPS - 1, 192, 128), vmem(REPS - 1, 448, 128)]
    scratch += [vmem(384, 128), vmem(896, 128)]
    scratch += [vmem(previous.shape[0], 2 * PANEL), vmem(REPS - 1, own_rows, 2 * PANEL)]
    dma = pltpu.SemaphoreType.DMA
    scratch += [
        dma((2, 2)), dma((2, 2, 3, SIDE - 1)), dma((2, 2, SIDE)),
        dma((2, 2, REPS - 1)), dma((2, 2)), dma((2, REPS - 1)),
    ]
    square = jax.ShapeDtypeStruct((PANEL, PANEL), f32)
    return pl.pallas_call(
        kernel,
        out_shape=(square, square, square, jax.ShapeDtypeStruct(columns.shape, f32)),
        in_specs=[pl.BlockSpec(memory_space=pltpu.VMEM)] * 3,
        out_specs=[pl.BlockSpec(memory_space=pltpu.VMEM)] * 4,
        scratch_shapes=scratch,
        compiler_params=pltpu.CompilerParams(collective_id=0, has_side_effects=True),
    )(pivots, previous, columns)


def per_device(pivots, previous, columns, diagonal):
    g11, g21, g22, resid = communicate(pivots, previous, columns)
    return factorise(g11, g21, g22, resid, diagonal)


def solution(mesh):
    placed = (P(), P("rows", "rep"), P(("rows", "rep"), None), P(("rows", "rep")))
    return jax.shard_map(
        per_device,
        mesh=mesh,
        in_specs=placed,
        out_specs=(P(("rows", "rep"), None), P(("rows", "rep"))),
        check_vma=False,
    )
```

```python
import functools

import jax
import jax.numpy as jnp
from jax import lax
from jax.experimental import pallas as pl
from jax.experimental.pallas import tpu as pltpu
from jax.sharding import PartitionSpec as P

HIGHEST = lax.Precision.HIGHEST
MESH = pl.DeviceIdType.MESH
BLOCK = 128
BLOCKS = 4
HALF = BLOCK // 2
EARLY = 384
SIDE = 8
REPS = 4
CHUNK = HALF // SIDE
WIDTHS = tuple(EARLY + BLOCK * (s + 1) for s in range(BLOCKS))
ORDER = (4, 3, 5, 2, 6, 1, 7)
BASE = 32
TILES = BASE // 8


def dot_tn(left, right):
    return lax.dot_general(
        left, right, (((0,), (0,)), ((), ())), precision=HIGHEST, preferred_element_type=jnp.float32
    )


def spread(tile, row):
    return jnp.broadcast_to(tile[row:row + 1, :], tile.shape)


def eliminate(square, wide):
    sub = lax.broadcasted_iota(jnp.int32, (8, 128), 0)
    cols = []
    for k in range(BASE):
        cols.append([None] * TILES)
        for v in range(k // 8, TILES):
            cols[k][v] = jnp.broadcast_to(square[8 * v:8 * v + 8, k:k + 1], (8, 128))
    lanes = wide.shape[1] // 128
    work = [[wide[8 * v:8 * v + 8, 128 * l:128 * l + 128] for l in range(lanes)] for v in range(TILES)]
    pivots = []
    for j in range(BASE):
        top, row = j // 8, j % 8
        pivot = spread(cols[j][top], row)
        pivots.append(pivot)
        inverse = 1.0 / pivot
        factor = [None] * TILES
        for v in range(top, TILES):
            value = cols[j][v] * inverse
            factor[v] = jnp.where(sub > row, value, 0.0) if v == top else value
        for k in range(j + 1, BASE):
            value = spread(cols[j][k // 8], k % 8)
            for v in range(k // 8, TILES):
                cols[k][v] = cols[k][v] - factor[v] * value
        for l in range(lanes):
            value = spread(work[top][l], row)
            for v in range(top, TILES):
                work[v][l] = work[v][l] - factor[v] * value
    out = []
    for v in range(TILES):
        pivot = pivots[8 * v]
        for s in range(1, 8):
            pivot = jnp.where(sub == s, pivots[8 * v + s], pivot)
        scale = lax.rsqrt(pivot)
        scale = scale * (1.5 - 0.5 * pivot * scale * scale)
        out.append(jnp.concatenate([work[v][l] * scale for l in range(lanes)], axis=1))
    return jnp.concatenate(out, axis=0)


def dot_nt(left, right, precision=HIGHEST):
    return lax.dot_general(
        left, right, (((1,), (1,)), ((), ())), precision=precision, preferred_element_type=jnp.float32
    )


def split(values):
    parts = []
    for _ in range(3):
        part = values.astype(jnp.bfloat16)
        values = values - part.astype(jnp.float32)
        parts.append(part)
    return parts


def pick(mask, parts):
    total = None
    for part in parts:
        term = lax.dot_general(mask, part, (((0,), (0,)), ((), ())), preferred_element_type=jnp.float32)
        total = term if total is None else total + term
    return total


def block_cols(s):
    return slice(s * BLOCK, s * BLOCK + BLOCK)


def kernel(pivots_ref, previous_ref, columns_ref, diagonal_ref, vectors_ref, diag_ref, *scratch):
    picks, pairs, halves, firsts, owns, seconds, fulls, gparts, gxs, gsums, partials, rress = (
        scratch[BLOCKS * n:BLOCKS * n + BLOCKS] for n in range(12)
    )
    prev_parts, col_parts, stash, upper, lower, inverse = scratch[12 * BLOCKS:12 * BLOCKS + 6]
    pair_sems, axis_sems, fwd_sems, gx_sems, gpair_sems, res_sems = scratch[12 * BLOCKS + 6:]
    rows = lax.axis_index("rows")
    rep = lax.axis_index("rep")
    core = lax.rem(rows, 2)
    chip_z = lax.rem(rows // 2, SIDE)
    chip_y = rows // (2 * SIDE)
    spot = (1 - core) * chip_y + core * chip_z
    block_rows = previous_ref.shape[0]
    own_rows = columns_ref.shape[0]

    def at(y, z, c):
        return (y * SIDE + z) * 2 + c

    def first_peer(d):
        y = lax.rem(chip_y + (1 - core) * d, SIDE)
        z = lax.rem(chip_z + core * d, SIDE)
        return at(y, z, core), lax.rem(spot + d, SIDE)

    def second_peer(d):
        y = lax.rem(chip_y + core * d, SIDE)
        z = lax.rem(chip_z + (1 - core) * d, SIDE)
        return at(y, z, core)

    partner = at(chip_y, chip_z, 1 - core)
    barrier = pltpu.get_barrier_semaphore()
    for d in range(1, SIDE):
        pl.semaphore_signal(barrier, inc=1, device_id=(first_peer(d)[0], rep), device_id_type=MESH)
        pl.semaphore_signal(barrier, inc=1, device_id=(second_peer(d), rep), device_id_type=MESH)
    for d in range(1, REPS):
        pl.semaphore_signal(barrier, inc=1, device_id=(rows, lax.rem(rep + d, REPS)), device_id_type=MESH)
    pl.semaphore_signal(barrier, inc=1, device_id=(partner, rep), device_id_type=MESH)

    def send(src, dst, sems, slot, where):
        copy = pltpu.make_async_remote_copy(
            src_ref=src, dst_ref=dst, send_sem=sems.at[(0,) + slot], recv_sem=sems.at[(1,) + slot],
            device_id=where, device_id_type=MESH,
        )
        copy.start()
        return copy

    flying = {}

    def make_parts():
        for n, part in enumerate(split(previous_ref[...])):
            prev_parts[n] = part
        pad = jnp.zeros((BLOCK - own_rows, BLOCKS * BLOCK), jnp.float32)
        for n, part in enumerate(split(jnp.concatenate([columns_ref[...], pad], axis=0))):
            col_parts[n] = part

    def make_picks(s):
        index = pivots_ref[s // 2:s // 2 + 1, block_cols(s % 2)]
        block = lax.broadcasted_iota(jnp.int32, (block_rows, BLOCK), 0) + rows * block_rows
        mask = jnp.where(block == index, 1.0, 0.0).astype(jnp.bfloat16)
        picks[s][:, :EARLY] = pick(mask, [prev_parts[n] for n in range(3)])
        place = lax.broadcasted_iota(jnp.int32, (BLOCK, BLOCK), 0)
        own = place + (rows * REPS + rep) * own_rows
        mask = jnp.where((own == index) & (place < own_rows), 1.0, 0.0).astype(jnp.bfloat16)
        wide = (s + 1 + (s + 1) % 2) * BLOCK
        found = pick(mask, [col_parts[n, :, :wide] for n in range(3)])
        same = found[:, block_cols(s)]
        same = 0.5 * (same + same.T)
        if s % 2 == 0:
            stash[s // 2] = found[:, block_cols(s + 1)]
            if s:
                picks[s][:, EARLY:EARLY + s * BLOCK] = found[:, :s * BLOCK]
        else:
            if s > 1:
                picks[s][:, EARLY:EARLY + (s - 1) * BLOCK] = found[:, :(s - 1) * BLOCK]
            mid = 0.5 * (found[:, block_cols(s - 1)] + stash[s // 2].T)
            picks[s][:, EARLY + (s - 1) * BLOCK:EARLY + s * BLOCK] = mid
        picks[s][:, EARLY + s * BLOCK:] = same

    def pair(s):
        src = picks[s].at[pl.ds((1 - core) * HALF, HALF), :]
        flying["pair", s] = send(src, pairs[s], pair_sems, (s,), (partner, rep))

    def first(s):
        flying["pair", s].wait()
        halves[s][...] = picks[s][pl.ds(core * HALF, HALF), :] + pairs[s][...]
        flying["first", s] = []
        for d in ORDER:
            peer, place = first_peer(d)
            src = halves[s].at[pl.ds(place * CHUNK, CHUNK), :]
            flying["first", s].append(send(src, firsts[s].at[d - 1], axis_sems, (s, 0, d - 1), (peer, rep)))

    def second(s):
        total = halves[s][pl.ds(spot * CHUNK, CHUNK), :]
        for copy in flying["first", s]:
            copy.wait()
        for d in range(1, SIDE):
            total = total + firsts[s][d - 1]
        owns[s][0] = total
        flying["second", s] = []
        for d in ORDER:
            where = (second_peer(d), rep)
            flying["second", s].append(send(owns[s].at[0], seconds[s].at[d - 1], axis_sems, (s, 1, d - 1), where))

    def gather(s):
        for copy in flying["second", s]:
            copy.wait()
        total = owns[s][0]
        for d in range(1, SIDE):
            total = total + seconds[s][d - 1]
        owns[s][1] = total
        place = pl.ds(core * HALF + spot * CHUNK, CHUNK)
        fulls[s][place, :] = total
        flying["gather", s] = {}
        for d in ORDER:
            where = (first_peer(d)[0], rep)
            flying["gather", s][d] = send(owns[s].at[1], fulls[s].at[place, :], axis_sems, (s, 2, d - 1), where)
        flying["gather", s][0] = send(owns[s].at[1], fulls[s].at[place, :], fwd_sems, (s, 0), (partner, rep))

    def forward(s):
        flying["forward", s] = []
        for d in (1, 7, 2, 6, 3, 5, 4):
            flying["gather", s][d].wait()
            source = lax.rem(spot + SIDE - d, SIDE)
            place = pl.ds(core * HALF + source * CHUNK, CHUNK)
            here = fulls[s].at[place, :]
            flying["forward", s].append(send(here, here, fwd_sems, (s, d), (partner, rep)))

    def gsum(s):
        flying["gather", s][0].wait()
        for copy in flying["forward", s]:
            copy.wait()
        chosen = fulls[s][:, :EARLY]
        for t in range(s + 1):
            found = fulls[s][:, EARLY + t * BLOCK:EARLY + t * BLOCK + BLOCK]
            gparts[s][:, block_cols(t)] = found - dot_nt(chosen, fulls[t][:, :EARLY])
        mine = pl.ds(core * HALF, HALF)
        flying["gsum", s] = []
        for d in (2, 1, 3):
            where = (rows, lax.rem(rep + d, REPS))
            flying["gsum", s].append(send(gparts[s].at[mine, :], gxs[s].at[d - 1], gx_sems, (s, d - 1), where))

    def gpair(s):
        mine = pl.ds(core * HALF, HALF)
        for copy in flying["gsum", s]:
            copy.wait()
        gsums[s][mine, :] = gparts[s][mine, :] + gxs[s][0] + gxs[s][1] + gxs[s][2]
        flying["gpair", s] = send(gsums[s].at[mine, :], gsums[s].at[mine, :], gpair_sems, (s,), (partner, rep))

    def scatter(s):
        partials[s][...] = dot_nt(previous_ref[...], fulls[s][:, :EARLY])
        flying["scatter", s] = []
        for d in (2, 1, 3):
            other = lax.rem(rep + d, REPS)
            src = partials[s].at[pl.ds(other * own_rows, own_rows), :]
            flying["scatter", s].append(send(src, rress[s].at[d - 1], res_sems, (s, d - 1), (rows, other)))

    def resid(s):
        for copy in flying["scatter", s]:
            copy.wait()
        mine = partials[s][pl.ds(rep * own_rows, own_rows), :]
        total = columns_ref[:, block_cols(s)] - (((mine + rress[s][0]) + rress[s][1]) + rress[s][2])
        for u in range(s):
            total = total - dot_nt(vectors_ref[:, block_cols(u)], lower[s, :, block_cols(u)])
        vectors_ref[:, block_cols(s)] = total

    def solve(s):
        vectors_ref[:, block_cols(s)] = dot_nt(vectors_ref[:, block_cols(s)], inverse[s])

    def factor(s, gaps):
        flying["gpair", s].wait()
        block = gsums[s][:, block_cols(s)]
        for t in range(s):
            row = gsums[s][:, block_cols(t)]
            for u in range(t):
                row = row - dot_nt(lower[s, :, block_cols(u)], lower[t, :, block_cols(u)])
            row = dot_nt(row, inverse[t])
            lower[s, :, block_cols(t)] = row
            block = block - dot_nt(row, row)
        gparts[s][:, block_cols(s)] = block
        for k in range(BLOCK // BASE):
            here = slice(k * BASE, k * BASE + BASE)
            lane = lax.broadcasted_iota(jnp.int32, (BASE, BLOCK), 1)
            sub = lax.broadcasted_iota(jnp.int32, (BASE, BLOCK), 0)
            eye = jnp.where(lane == sub + k * BASE, 1.0, 0.0)
            wide = jnp.concatenate([gparts[s][here, block_cols(s)], eye], axis=1)
            for done in (slice(0, (k - 1) * BASE), slice(max(k - 1, 0) * BASE, k * BASE)):
                if done.stop > done.start:
                    wide = wide - dot_tn(upper[done, here], upper[done, :])
            upper[here, :] = eliminate(wide[:, here], wide)
            if k == BLOCK // BASE - 1:
                inverse[s] = upper[:, BLOCK:]
            for step in gaps.get(k, ()):
                step()

    def later(work, s):
        return lambda: work(s)

    make_parts()
    make_picks(0)
    pl.semaphore_wait(barrier, 2 * (SIDE - 1) + REPS)
    pair(0)
    make_picks(1)
    first(0)
    pair(1)
    make_picks(2)
    make_picks(3)
    second(0)
    first(1)
    pair(2)
    gather(0)
    second(1)
    forward(0)
    gsum(0)
    gather(1)
    first(2)
    pair(3)
    gpair(0)
    forward(1)
    gsum(1)
    second(2)
    factor(0, {
        0: (later(gpair, 1), later(first, 3)),
        1: (later(gather, 2), later(scatter, 0)),
        2: (later(second, 3), later(forward, 2)),
        3: (later(gsum, 2), later(scatter, 1)),
    })
    factor(1, {
        0: (later(gather, 3), later(resid, 0), later(solve, 0)),
        1: (later(gpair, 2),),
        2: (later(forward, 3), later(resid, 1)),
        3: (later(gsum, 3), later(solve, 1)),
    })
    factor(2, {
        0: (later(scatter, 2),),
        1: (later(gpair, 3),),
        2: (later(scatter, 3),),
        3: (later(resid, 2), later(solve, 2)),
    })
    factor(3, {3: (later(resid, 3), later(solve, 3))})
    ones = jnp.ones((8, BLOCK), jnp.float32)
    sums = diagonal_ref[...]
    for s in range(BLOCKS):
        vec = vectors_ref[:, block_cols(s)]
        sums = sums - dot_nt(ones, vec * vec)[0:1, :]
    diag_ref[...] = sums


def per_device(pivots, previous, columns, diagonal):
    f32 = jnp.float32
    own_rows = columns.shape[0]
    block_rows = previous.shape[0]
    vmem = lambda *shape: pltpu.VMEM(shape, f32)
    each = lambda build: [build(s) for s in range(BLOCKS)]
    scratch = []
    scratch += each(lambda s: vmem(BLOCK, WIDTHS[s]))
    scratch += each(lambda s: vmem(HALF, WIDTHS[s]))
    scratch += each(lambda s: vmem(HALF, WIDTHS[s]))
    scratch += each(lambda s: vmem(SIDE - 1, CHUNK, WIDTHS[s]))
    scratch += each(lambda s: vmem(2, CHUNK, WIDTHS[s]))
    scratch += each(lambda s: vmem(SIDE - 1, CHUNK, WIDTHS[s]))
    scratch += each(lambda s: vmem(BLOCK, WIDTHS[s]))
    scratch += each(lambda s: vmem(BLOCK, BLOCK * (s + 1)))
    scratch += each(lambda s: vmem(REPS - 1, HALF, BLOCK * (s + 1)))
    scratch += each(lambda s: vmem(BLOCK, BLOCK * (s + 1)))
    scratch += each(lambda s: vmem(block_rows, BLOCK))
    scratch += each(lambda s: vmem(REPS - 1, own_rows, BLOCK))
    scratch += [
        pltpu.VMEM((3, block_rows, EARLY), jnp.bfloat16), pltpu.VMEM((3, BLOCK, BLOCKS * BLOCK), jnp.bfloat16),
        vmem(2, BLOCK, BLOCK), vmem(BLOCK, 2 * BLOCK), vmem(BLOCKS, BLOCK, BLOCKS * BLOCK), vmem(BLOCKS, BLOCK, BLOCK),
    ]
    dma = pltpu.SemaphoreType.DMA
    scratch += [
        dma((2, BLOCKS)), dma((2, BLOCKS, 3, SIDE - 1)), dma((2, BLOCKS, SIDE)),
        dma((2, BLOCKS, REPS - 1)), dma((2, BLOCKS)), dma((2, BLOCKS, REPS - 1)),
    ]
    space = pl.BlockSpec(memory_space=pltpu.VMEM)
    vectors, diag = pl.pallas_call(
        kernel,
        out_shape=(jax.ShapeDtypeStruct(columns.shape, f32), jax.ShapeDtypeStruct((1, own_rows), f32)),
        in_specs=[space] * 4,
        out_specs=[space] * 2,
        scratch_shapes=scratch,
        compiler_params=pltpu.CompilerParams(collective_id=0, has_side_effects=True),
    )(pivots, previous, columns, diagonal.reshape(1, own_rows))
    return vectors, diag.reshape(own_rows)


def solution(mesh):
    placed = (P(), P("rows", "rep"), P(("rows", "rep"), None), P(("rows", "rep")))
    return jax.shard_map(
        per_device,
        mesh=mesh,
        in_specs=placed,
        out_specs=(P(("rows", "rep"), None), P(("rows", "rep"))),
        check_vma=False,
    )
```

```python
import functools

import jax
import jax.numpy as jnp
from jax import lax
from jax.experimental import pallas as pl
from jax.experimental.pallas import tpu as pltpu
from jax.sharding import PartitionSpec as P

HIGHEST = lax.Precision.HIGHEST
MESH = pl.DeviceIdType.MESH
BLOCK = 128
BLOCKS = 4
HALF = BLOCK // 2
EARLY = 384
SIDE = 8
REPS = 4
COUNTS = (BLOCK, (BLOCKS - 1) * BLOCK, (BLOCKS - 1) * BLOCK)
LANES = (EARLY + BLOCK, EARLY, BLOCK)
ORDER = (4, 3, 5, 2, 6, 1, 7)
BASE = 32
TILES = BASE // 8


def dot_tn(left, right):
    return lax.dot_general(
        left, right, (((0,), (0,)), ((), ())), precision=HIGHEST, preferred_element_type=jnp.float32
    )


def spread(tile, row):
    return jnp.broadcast_to(tile[row:row + 1, :], tile.shape)


def eliminate(square, wide):
    sub = lax.broadcasted_iota(jnp.int32, (8, 128), 0)
    cols = []
    for k in range(BASE):
        cols.append([None] * TILES)
        for v in range(k // 8, TILES):
            cols[k][v] = jnp.broadcast_to(square[8 * v:8 * v + 8, k:k + 1], (8, 128))
    lanes = wide.shape[1] // 128
    work = [[wide[8 * v:8 * v + 8, 128 * l:128 * l + 128] for l in range(lanes)] for v in range(TILES)]
    pivots = []
    for j in range(BASE):
        top, row = j // 8, j % 8
        pivot = spread(cols[j][top], row)
        pivots.append(pivot)
        inverse = 1.0 / pivot
        factor = [None] * TILES
        for v in range(top, TILES):
            value = cols[j][v] * inverse
            factor[v] = jnp.where(sub > row, value, 0.0) if v == top else value
        for k in range(j + 1, BASE):
            value = spread(cols[j][k // 8], k % 8)
            for v in range(k // 8, TILES):
                cols[k][v] = cols[k][v] - factor[v] * value
        for l in range(lanes):
            value = spread(work[top][l], row)
            for v in range(top, TILES):
                work[v][l] = work[v][l] - factor[v] * value
    out = []
    for v in range(TILES):
        pivot = pivots[8 * v]
        for s in range(1, 8):
            pivot = jnp.where(sub == s, pivots[8 * v + s], pivot)
        scale = lax.rsqrt(pivot)
        scale = scale * (1.5 - 0.5 * pivot * scale * scale)
        out.append(jnp.concatenate([work[v][l] * scale for l in range(lanes)], axis=1))
    return jnp.concatenate(out, axis=0)


def dot_nt(left, right, precision=HIGHEST):
    return lax.dot_general(
        left, right, (((1,), (1,)), ((), ())), precision=precision, preferred_element_type=jnp.float32
    )


def split(values):
    parts = []
    for _ in range(3):
        part = values.astype(jnp.bfloat16)
        values = values - part.astype(jnp.float32)
        parts.append(part)
    return parts


def pick(mask, parts):
    total = None
    for part in parts:
        term = lax.dot_general(mask, part, (((0,), (0,)), ((), ())), preferred_element_type=jnp.float32)
        total = term if total is None else total + term
    return total


def block_cols(s):
    return slice(s * BLOCK, s * BLOCK + BLOCK)


def kernel(pivots_ref, previous_ref, columns_ref, diagonal_ref, vectors_ref, diag_ref, *scratch):
    picks, pairs, halves, firsts, owns, seconds, fulls = (scratch[3 * n:3 * n + 3] for n in range(7))
    scratch = scratch[21:]
    gparts, gxs, gaccs, gsums = (scratch[BLOCKS * n:BLOCKS * n + BLOCKS] for n in range(4))
    scratch = scratch[4 * BLOCKS:]
    partials, rress, raccs = scratch[:2], scratch[2:4], scratch[4:6]
    prev_parts, slices, extra, upper, lower, inverse, parts = scratch[6:13]
    swap_sems, pair_sems, axis_sems, fwd_sems, gx_sems, gpair_sems, res_sems = scratch[13:]
    rows = lax.axis_index("rows")
    rep = lax.axis_index("rep")
    core = lax.rem(rows, 2)
    chip_z = lax.rem(rows // 2, SIDE)
    chip_y = rows // (2 * SIDE)
    spot = (1 - core) * chip_y + core * chip_z
    block_rows = previous_ref.shape[0]
    own_rows = columns_ref.shape[0]

    def at(y, z, c):
        return (y * SIDE + z) * 2 + c

    def first_peer(d):
        y = lax.rem(chip_y + (1 - core) * d, SIDE)
        z = lax.rem(chip_z + core * d, SIDE)
        return at(y, z, core), lax.rem(spot + d, SIDE)

    def second_peer(d):
        y = lax.rem(chip_y + core * d, SIDE)
        z = lax.rem(chip_z + (1 - core) * d, SIDE)
        return at(y, z, core)

    partner = at(chip_y, chip_z, 1 - core)
    turn = (1 - 2 * lax.rem(rep, 2)) * (1 - 2 * core)
    near = lax.rem(rep + turn + REPS, REPS)
    next_near = lax.rem(rep - turn + REPS, REPS)
    opposite = lax.rem(rep + 2, REPS)
    barrier = pltpu.get_barrier_semaphore()
    for d in range(1, SIDE):
        pl.semaphore_signal(barrier, inc=1, device_id=(first_peer(d)[0], rep), device_id_type=MESH)
        pl.semaphore_signal(barrier, inc=1, device_id=(second_peer(d), rep), device_id_type=MESH)
    for d in range(1, REPS):
        pl.semaphore_signal(barrier, inc=1, device_id=(rows, lax.rem(rep + d, REPS)), device_id_type=MESH)
    pl.semaphore_signal(barrier, inc=1, device_id=(partner, rep), device_id_type=MESH)

    def send(src, dst, sems, slot, where):
        copy = pltpu.make_async_remote_copy(
            src_ref=src, dst_ref=dst, send_sem=sems.at[(0,) + slot], recv_sem=sems.at[(1,) + slot],
            device_id=where, device_id_type=MESH,
        )
        copy.start()
        return copy

    flying = {}

    def index_of(s):
        return pivots_ref[s // 2:s // 2 + 1, block_cols(s % 2)]

    def block_mask(index):
        place = lax.broadcasted_iota(jnp.int32, (block_rows, index.shape[1]), 0) + rows * block_rows
        return jnp.where(place == index, 1.0, 0.0).astype(jnp.bfloat16)

    def pick_first():
        for n, part in enumerate(split(previous_ref[...])):
            prev_parts[n] = part
        picks[0][:, :EARLY] = pick(block_mask(index_of(0)), [prev_parts[n] for n in range(3)])
        place = lax.broadcasted_iota(jnp.int32, (BLOCK, BLOCK), 0)
        own = place + (rows * REPS + rep) * own_rows
        mask = jnp.where((own == index_of(0)) & (place < own_rows), 1.0, 0.0).astype(jnp.bfloat16)
        pad = jnp.zeros((BLOCK - own_rows, BLOCK), jnp.float32)
        found = pick(mask, split(jnp.concatenate([columns_ref[:, :BLOCK], pad], axis=0)))
        picks[0][:, EARLY:] = 0.5 * (found + found.T)

    def swap():
        flying["swap"] = []
        here = pl.ds(rep * own_rows, own_rows)
        for d in (2, 1, 3):
            other = lax.rem(rep + d, REPS)
            src = columns_ref.at[:, pl.ds(pl.multiple_of(other * BLOCK, BLOCK), BLOCK)]
            flying["swap"].append(send(src, slices.at[here, :], swap_sems, (d - 1,), (rows, other)))
        slices[here, :] = columns_ref[:, pl.ds(pl.multiple_of(rep * BLOCK, BLOCK), BLOCK)]
        extra[here, :] = columns_ref[:, block_cols(1)]
        for d in (2, 1, 3):
            other = lax.rem(rep + d, REPS)

            @pl.when(other == 2)
            def _():
                send(columns_ref.at[:, block_cols(1)], extra.at[here, :], swap_sems, (d + 2,), (rows, other)).wait_send()

    def pick_rest_early():
        index = jnp.concatenate([index_of(s) for s in range(1, BLOCKS)], axis=1)
        picks[1][...] = pick(block_mask(index), [prev_parts[n] for n in range(3)])

    def pick_rest_late():
        for copy in flying["swap"]:
            copy.wait()

        @pl.when(rep == 2)
        def _():
            here = pl.ds(rep * own_rows, own_rows)
            for d in (2, 1, 3):
                pltpu.make_async_remote_copy(
                    src_ref=columns_ref.at[:, block_cols(1)], dst_ref=extra.at[here, :], send_sem=swap_sems.at[0, d + 2],
                    recv_sem=swap_sems.at[1, d + 2], device_id=(rows, lax.rem(rep + d, REPS)), device_id_type=MESH,
                ).wait_recv()

        found = jnp.where(rep == 2, extra[...], slices[...])
        picks[2][:BLOCK, :] = pick(block_mask(jnp.where(rep == 2, index_of(0), index_of(1))), split(found))
        index = jnp.concatenate([index_of(s) for s in range(2, BLOCKS)], axis=1)
        picks[2][BLOCK:, :] = pick(block_mask(index), split(slices[...]))

    def pair(s):
        half, chunk = COUNTS[s] // 2, COUNTS[s] // 2 // SIDE
        src = picks[s].at[pl.ds((1 - core) * half, half), :]
        flying["pair", s] = send(src, pairs[s], pair_sems, (s,), (partner, rep))

    def first(s):
        half, chunk = COUNTS[s] // 2, COUNTS[s] // 2 // SIDE
        flying["pair", s].wait()
        halves[s][...] = picks[s][pl.ds(core * half, half), :] + pairs[s][...]
        flying["first", s] = []
        for d in ORDER:
            peer, place = first_peer(d)
            src = halves[s].at[pl.ds(place * chunk, chunk), :]
            flying["first", s].append(send(src, firsts[s].at[d - 1], axis_sems, (s, 0, d - 1), (peer, rep)))

    def second(s):
        half, chunk = COUNTS[s] // 2, COUNTS[s] // 2 // SIDE
        total = halves[s][pl.ds(spot * chunk, chunk), :]
        for copy in flying["first", s]:
            copy.wait()
        for d in range(1, SIDE):
            total = total + firsts[s][d - 1]
        owns[s][0] = total
        flying["second", s] = []
        for d in ORDER:
            where = (second_peer(d), rep)
            flying["second", s].append(send(owns[s].at[0], seconds[s].at[d - 1], axis_sems, (s, 1, d - 1), where))

    def gather(s):
        half, chunk = COUNTS[s] // 2, COUNTS[s] // 2 // SIDE
        for copy in flying["second", s]:
            copy.wait()
        total = owns[s][0]
        for d in range(1, SIDE):
            total = total + seconds[s][d - 1]
        owns[s][1] = total
        place = pl.ds(core * half + spot * chunk, chunk)
        fulls[s][place, :] = total
        flying["gather", s] = {}
        for d in ORDER:
            where = (first_peer(d)[0], rep)
            flying["gather", s][d] = send(owns[s].at[1], fulls[s].at[place, :], axis_sems, (s, 2, d - 1), where)
        flying["gather", s][0] = send(owns[s].at[1], fulls[s].at[place, :], fwd_sems, (s, 0), (partner, rep))

    def forward(s):
        half, chunk = COUNTS[s] // 2, COUNTS[s] // 2 // SIDE
        flying["forward", s] = []
        for d in (1, 7, 2, 6, 3, 5, 4):
            flying["gather", s][d].wait()
            source = lax.rem(spot + SIDE - d, SIDE)
            place = pl.ds(core * half + source * chunk, chunk)
            here = fulls[s].at[place, :]
            flying["forward", s].append(send(here, here, fwd_sems, (s, d), (partner, rep)))

    def landed(s):
        flying["gather", s][0].wait()
        for copy in flying["forward", s]:
            copy.wait()
        if s < 2:
            where = slice(0, BLOCK) if s == 0 else slice(BLOCK, BLOCKS * BLOCK)
            for n, part in enumerate(split(fulls[s][:, :EARLY])):
                parts[n, where, :] = part

    def products(left, left_rows, right_rows, terms):
        total = None
        for a, b in terms:
            term = lax.dot_general(
                left[a, left_rows, :], parts[b, right_rows, :], (((1,), (1,)), ((), ())),
                preferred_element_type=jnp.float32,
            )
            total = term if total is None else total + term
        return total

    def slot(s):
        return fulls[0][:, EARLY:] if s == 0 else fulls[2][(s - 1) * BLOCK:s * BLOCK, :]

    def weighed(place, value):
        return jnp.where(rep == place, value, 0.0)

    def column_part(s, t):
        value = slot(s)
        if s == 0:
            return value
        if t == s:
            return weighed(t, 0.5 * (value + value.T))
        if s == 1:
            return 0.5 * (weighed(0, value) + weighed(2, value.T))
        if (s, t) == (3, 2):
            return 0.5 * (weighed(2, value) + weighed(3, slot(2).T))
        return weighed(t, value)

    def gsum(s):
        terms = ((1, 1), (0, 2), (2, 0), (0, 1), (1, 0), (0, 0))
        gram = products(parts, block_cols(s), slice(0, s * BLOCK + BLOCK), terms)
        for t in range(s + 1):
            gparts[s][:, block_cols(t)] = column_part(s, t) - gram[:, block_cols(t)]
        mine = pl.ds(core * HALF, HALF)
        flying["gsum", s] = send(gparts[s].at[mine, :], gxs[s].at[0], gx_sems, (s, 0), (rows, near))

    def gnext(s):
        flying["gsum", s].wait()
        gaccs[s][...] = gparts[s][pl.ds(core * HALF, HALF), :] + gxs[s][0]
        flying["gnext", s] = send(gaccs[s].at[:, :], gxs[s].at[1], gx_sems, (s, 1), (rows, next_near))

    def gpair(s):
        mine = pl.ds(core * HALF, HALF)
        flying["gnext", s].wait()
        gsums[s][mine, :] = gaccs[s][...] + gxs[s][1]
        flying["gpair", s] = send(gsums[s].at[mine, :], gsums[s].at[mine, :], gpair_sems, (s,), (partner, rep))

    def rows_of(place):
        return pl.ds(place * own_rows, own_rows)

    def multiply(n):
        where = slice(0, BLOCK) if n == 0 else slice(BLOCK, BLOCKS * BLOCK)
        partials[n][...] = products(prev_parts, slice(None), where, ((0, 1), (1, 0), (0, 0)))

    def scatter(n):
        flying["scatter", n] = [
            send(partials[n].at[rows_of(place), :], rress[n].at[slot_of], res_sems, (n, slot_of), (rows, near))
            for slot_of, place in ((1, opposite), (0, near))
        ]

    def scatter_next(n):
        for copy in flying["scatter", n]:
            copy.wait()
        raccs[n][...] = partials[n][rows_of(next_near), :] + rress[n][1]
        flying["scatter_next", n] = send(raccs[n].at[:, :], rress[n].at[2], res_sems, (n, 2), (rows, next_near))

    def collect(n):
        flying["scatter_next", n].wait()
        total = (partials[n][rows_of(rep), :] + rress[n][0]) + rress[n][2]
        lanes = slice(0, BLOCK) if n == 0 else slice(BLOCK, BLOCKS * BLOCK)
        vectors_ref[:, lanes] = columns_ref[:, lanes] - total

    def update(s, t):
        done = dot_nt(vectors_ref[:, block_cols(t)], lower[s, :, block_cols(t)])
        vectors_ref[:, block_cols(s)] = vectors_ref[:, block_cols(s)] - done

    def solve(s):
        vectors_ref[:, block_cols(s)] = dot_nt(vectors_ref[:, block_cols(s)], inverse[s])

    def prepare(s, t):
        row = dot_nt(gsums[s][:, block_cols(t)], inverse[t])
        lower[s, :, block_cols(t)] = row
        for u in range(t + 1, s + 1):
            other = row if u == s else lower[u, :, block_cols(t)]
            gsums[s][:, block_cols(u)] = gsums[s][:, block_cols(u)] - dot_nt(row, other)

    def arrive(s):
        flying["gpair", s].wait()

    def factor(s, gaps):
        for k in range(BLOCK // BASE):
            here = slice(k * BASE, k * BASE + BASE)
            lane = lax.broadcasted_iota(jnp.int32, (BASE, BLOCK), 1)
            sub = lax.broadcasted_iota(jnp.int32, (BASE, BLOCK), 0)
            eye = jnp.where(lane == sub + k * BASE, 1.0, 0.0)
            wide = jnp.concatenate([gsums[s][here, block_cols(s)], eye], axis=1)
            for done in (slice(0, (k - 1) * BASE), slice(max(k - 1, 0) * BASE, k * BASE)):
                if done.stop > done.start:
                    wide = wide - dot_tn(upper[done, here], upper[done, :])
            for step in gaps.get(k, ()):
                step()
            upper[here, :] = eliminate(wide[:, here], wide)
        inverse[s] = upper[:, BLOCK:]

    def later(work, *which):
        return lambda: work(*which)

    pick_first()
    pick_rest_early()
    pl.semaphore_wait(barrier, 2 * (SIDE - 1) + REPS)
    pair(0)
    pair(1)
    swap()
    first(0)
    first(1)
    pick_rest_late()
    pair(2)
    second(0)
    first(2)
    second(1)
    gather(0)
    second(2)
    forward(0)
    landed(0)
    gsum(0)
    gather(1)
    gather(2)
    gnext(0)
    multiply(0)
    gpair(0)
    scatter(0)
    arrive(0)
    forward(1)
    forward(2)
    landed(1)
    landed(2)
    gsum(1)
    gsum(2)
    gsum(3)
    scatter_next(0)
    factor(0, {})
    gnext(1)
    gnext(2)
    gnext(3)
    gpair(1)
    multiply(1)
    scatter(1)
    collect(0)
    solve(0)
    arrive(1)
    prepare(1, 0)
    factor(1, {
        0: (later(gpair, 2),),
        1: (later(gpair, 3),),
        2: (later(arrive, 2), later(prepare, 2, 0)),
    })
    prepare(2, 1)
    factor(2, {
        0: (later(scatter_next, 1), later(arrive, 3), later(prepare, 3, 0)),
        1: (later(prepare, 3, 1),),
        3: (later(collect, 1), later(update, 1, 0)),
    })
    prepare(3, 2)
    factor(3, {
        0: (later(solve, 1), later(update, 2, 0)),
        1: (later(update, 2, 1), later(update, 3, 0)),
        2: (later(solve, 2), later(update, 3, 1)),
        3: (later(update, 3, 2),),
    })
    solve(3)
    ones = jnp.ones((8, BLOCK), jnp.float32)
    sums = diagonal_ref[...]
    for s in range(BLOCKS):
        vec = vectors_ref[:, block_cols(s)]
        sums = sums - dot_nt(ones, vec * vec)[0:1, :]
    diag_ref[...] = sums


def per_device(pivots, previous, columns, diagonal):
    f32 = jnp.float32
    own_rows = columns.shape[0]
    block_rows = previous.shape[0]
    vmem = lambda *shape: pltpu.VMEM(shape, f32)
    each = lambda build: [build(s) for s in range(BLOCKS)]
    scratch = []
    for build in (
        lambda n, w: vmem(n, w), lambda n, w: vmem(n // 2, w), lambda n, w: vmem(n // 2, w),
        lambda n, w: vmem(SIDE - 1, n // 2 // SIDE, w), lambda n, w: vmem(2, n // 2 // SIDE, w),
        lambda n, w: vmem(SIDE - 1, n // 2 // SIDE, w), lambda n, w: vmem(n, w),
    ):
        scratch += [build(n, w) for n, w in zip(COUNTS, LANES)]
    scratch += each(lambda s: vmem(BLOCK, BLOCK * (s + 1)))
    scratch += each(lambda s: vmem(2, HALF, BLOCK * (s + 1)))
    scratch += each(lambda s: vmem(HALF, BLOCK * (s + 1)))
    scratch += each(lambda s: vmem(BLOCK, BLOCK * (s + 1)))
    scratch += [vmem(block_rows, n) for n in COUNTS[:2]]
    scratch += [vmem(REPS - 1, own_rows, n) for n in COUNTS[:2]]
    scratch += [vmem(own_rows, n) for n in COUNTS[:2]]
    scratch += [
        pltpu.VMEM((3, block_rows, EARLY), jnp.bfloat16), vmem(block_rows, BLOCK), vmem(block_rows, BLOCK),
        vmem(BLOCK, 2 * BLOCK), vmem(BLOCKS, BLOCK, BLOCKS * BLOCK), vmem(BLOCKS, BLOCK, BLOCK),
        pltpu.VMEM((3, BLOCKS * BLOCK, EARLY), jnp.bfloat16),
    ]
    dma = pltpu.SemaphoreType.DMA
    scratch += [
        dma((2, 2 * (REPS - 1))), dma((2, 3)), dma((2, 3, 3, SIDE - 1)), dma((2, 3, SIDE)),
        dma((2, BLOCKS, 2)), dma((2, BLOCKS)), dma((2, 2, REPS - 1)),
    ]
    space = pl.BlockSpec(memory_space=pltpu.VMEM)
    vectors, diag = pl.pallas_call(
        kernel,
        out_shape=(jax.ShapeDtypeStruct(columns.shape, f32), jax.ShapeDtypeStruct((1, own_rows), f32)),
        in_specs=[space] * 4,
        out_specs=[space] * 2,
        scratch_shapes=scratch,
        compiler_params=pltpu.CompilerParams(collective_id=0, has_side_effects=True),
    )(pivots, previous, columns, diagonal.reshape(1, own_rows))
    return vectors, diag.reshape(own_rows)


def solution(mesh):
    placed = (P(), P("rows", "rep"), P(("rows", "rep"), None), P(("rows", "rep")))
    return jax.shard_map(
        per_device,
        mesh=mesh,
        in_specs=placed,
        out_specs=(P(("rows", "rep"), None), P(("rows", "rep"))),
        check_vma=False,
    )
```

```python
import functools

import jax
import jax.numpy as jnp
from jax import lax
from jax.experimental import pallas as pl
from jax.experimental.pallas import tpu as pltpu
from jax.sharding import PartitionSpec as P

HIGHEST = lax.Precision.HIGHEST
MESH = pl.DeviceIdType.MESH
BLOCK = 128
BLOCKS = 4
HALF = BLOCK // 2
EARLY = 384
SIDE = 8
REPS = 4
COUNTS = (BLOCK, (BLOCKS - 1) * BLOCK, (BLOCKS - 1) * BLOCK)
LANES = (EARLY + BLOCK, EARLY, BLOCK)
ORDER = (4, 3, 5, 2, 6, 1, 7)
BASE = 32
TILES = BASE // 8


def dot_tn(left, right):
    return lax.dot_general(
        left, right, (((0,), (0,)), ((), ())), precision=HIGHEST, preferred_element_type=jnp.float32
    )


def spread(tile, row):
    return jnp.broadcast_to(tile[row:row + 1, :], tile.shape)


def eliminate(square, wide):
    sub = lax.broadcasted_iota(jnp.int32, (8, 128), 0)
    cols = []
    for k in range(BASE):
        cols.append([None] * TILES)
        for v in range(k // 8, TILES):
            cols[k][v] = jnp.broadcast_to(square[8 * v:8 * v + 8, k:k + 1], (8, 128))
    lanes = wide.shape[1] // 128
    work = [[wide[8 * v:8 * v + 8, 128 * l:128 * l + 128] for l in range(lanes)] for v in range(TILES)]
    pivots = []
    for j in range(BASE):
        top, row = j // 8, j % 8
        pivot = spread(cols[j][top], row)
        pivots.append(pivot)
        inverse = 1.0 / pivot
        factor = [None] * TILES
        for v in range(top, TILES):
            value = cols[j][v] * inverse
            factor[v] = jnp.where(sub > row, value, 0.0) if v == top else value
        for k in range(j + 1, BASE):
            value = spread(cols[j][k // 8], k % 8)
            for v in range(k // 8, TILES):
                cols[k][v] = cols[k][v] - factor[v] * value
        for l in range(lanes):
            value = spread(work[top][l], row)
            for v in range(top, TILES):
                work[v][l] = work[v][l] - factor[v] * value
    out = []
    for v in range(TILES):
        pivot = pivots[8 * v]
        for s in range(1, 8):
            pivot = jnp.where(sub == s, pivots[8 * v + s], pivot)
        scale = lax.rsqrt(pivot)
        scale = scale * (1.5 - 0.5 * pivot * scale * scale)
        out.append(jnp.concatenate([work[v][l] * scale for l in range(lanes)], axis=1))
    return jnp.concatenate(out, axis=0)


def dot_nt(left, right, precision=HIGHEST):
    return lax.dot_general(
        left, right, (((1,), (1,)), ((), ())), precision=precision, preferred_element_type=jnp.float32
    )


def split(values):
    parts = []
    for _ in range(3):
        part = values.astype(jnp.bfloat16)
        values = values - part.astype(jnp.float32)
        parts.append(part)
    return parts


def pick(mask, parts):
    total = None
    for part in parts:
        term = lax.dot_general(mask, part, (((0,), (0,)), ((), ())), preferred_element_type=jnp.float32)
        total = term if total is None else total + term
    return total


def block_cols(s):
    return slice(s * BLOCK, s * BLOCK + BLOCK)


def kernel(pivots_ref, previous_ref, columns_ref, diagonal_ref, vectors_ref, diag_ref, *scratch):
    picks, pairs, halves, firsts, owns, seconds, fulls = (scratch[3 * n:3 * n + 3] for n in range(7))
    scratch = scratch[21:]
    gparts, gxs, gaccs, gsums = (scratch[BLOCKS * n:BLOCKS * n + BLOCKS] for n in range(4))
    scratch = scratch[4 * BLOCKS:]
    partials, rress, raccs = scratch[:2], scratch[2:4], scratch[4:6]
    prev_parts, slices, extra, upper, lower, inverse, parts = scratch[6:13]
    swap_sems, pair_sems, axis_sems, fwd_sems, gx_sems, gpair_sems, res_sems = scratch[13:]
    rows = lax.axis_index("rows")
    rep = lax.axis_index("rep")
    core = lax.rem(rows, 2)
    chip_z = lax.rem(rows // 2, SIDE)
    chip_y = rows // (2 * SIDE)
    spot = (1 - core) * chip_y + core * chip_z
    block_rows = previous_ref.shape[0]
    own_rows = columns_ref.shape[0]

    def at(y, z, c):
        return (y * SIDE + z) * 2 + c

    def first_peer(d):
        y = lax.rem(chip_y + (1 - core) * d, SIDE)
        z = lax.rem(chip_z + core * d, SIDE)
        return at(y, z, core), lax.rem(spot + d, SIDE)

    def second_peer(d):
        y = lax.rem(chip_y + core * d, SIDE)
        z = lax.rem(chip_z + (1 - core) * d, SIDE)
        return at(y, z, core)

    partner = at(chip_y, chip_z, 1 - core)
    turn = (1 - 2 * lax.rem(rep, 2)) * (1 - 2 * core)
    near = lax.rem(rep + turn + REPS, REPS)
    next_near = lax.rem(rep - turn + REPS, REPS)
    opposite = lax.rem(rep + 2, REPS)
    barrier = pltpu.get_barrier_semaphore()
    for d in range(1, SIDE):
        pl.semaphore_signal(barrier, inc=1, device_id=(first_peer(d)[0], rep), device_id_type=MESH)
        pl.semaphore_signal(barrier, inc=1, device_id=(second_peer(d), rep), device_id_type=MESH)
    for d in range(1, REPS):
        pl.semaphore_signal(barrier, inc=1, device_id=(rows, lax.rem(rep + d, REPS)), device_id_type=MESH)
    pl.semaphore_signal(barrier, inc=1, device_id=(partner, rep), device_id_type=MESH)

    def send(src, dst, sems, slot, where):
        copy = pltpu.make_async_remote_copy(
            src_ref=src, dst_ref=dst, send_sem=sems.at[(0,) + slot], recv_sem=sems.at[(1,) + slot],
            device_id=where, device_id_type=MESH,
        )
        copy.start()
        return copy

    flying = {}

    def index_of(s):
        return pivots_ref[s // 2:s // 2 + 1, block_cols(s % 2)]

    def block_mask(index):
        place = lax.broadcasted_iota(jnp.int32, (block_rows, index.shape[1]), 0) + rows * block_rows
        return jnp.where(place == index, 1.0, 0.0).astype(jnp.bfloat16)

    def pick_first():
        for n, part in enumerate(split(previous_ref[...])):
            prev_parts[n] = part
        picks[0][:, :EARLY] = pick(block_mask(index_of(0)), [prev_parts[n] for n in range(3)])
        place = lax.broadcasted_iota(jnp.int32, (BLOCK, BLOCK), 0)
        own = place + (rows * REPS + rep) * own_rows
        mask = jnp.where((own == index_of(0)) & (place < own_rows), 1.0, 0.0).astype(jnp.bfloat16)
        pad = jnp.zeros((BLOCK - own_rows, BLOCK), jnp.float32)
        found = pick(mask, split(jnp.concatenate([columns_ref[:, :BLOCK], pad], axis=0)))
        picks[0][:, EARLY:] = 0.5 * (found + found.T)

    def swap():
        flying["swap"] = []
        here = pl.ds(rep * own_rows, own_rows)
        for d in (2, 1, 3):
            other = lax.rem(rep + d, REPS)
            src = columns_ref.at[:, pl.ds(pl.multiple_of(other * BLOCK, BLOCK), BLOCK)]
            flying["swap"].append(send(src, slices.at[here, :], swap_sems, (d - 1,), (rows, other)))
        slices[here, :] = columns_ref[:, pl.ds(pl.multiple_of(rep * BLOCK, BLOCK), BLOCK)]
        extra[here, :] = columns_ref[:, block_cols(1)]
        for d in (2, 1, 3):
            other = lax.rem(rep + d, REPS)

            @pl.when(other == 2)
            def _():
                send(columns_ref.at[:, block_cols(1)], extra.at[here, :], swap_sems, (d + 2,), (rows, other)).wait_send()

    def pick_rest_early():
        index = jnp.concatenate([index_of(s) for s in range(1, BLOCKS)], axis=1)
        picks[1][...] = pick(block_mask(index), [prev_parts[n] for n in range(3)])

    def pick_rest_late():
        for copy in flying["swap"]:
            copy.wait()

        @pl.when(rep == 2)
        def _():
            here = pl.ds(rep * own_rows, own_rows)
            for d in (2, 1, 3):
                pltpu.make_async_remote_copy(
                    src_ref=columns_ref.at[:, block_cols(1)], dst_ref=extra.at[here, :], send_sem=swap_sems.at[0, d + 2],
                    recv_sem=swap_sems.at[1, d + 2], device_id=(rows, lax.rem(rep + d, REPS)), device_id_type=MESH,
                ).wait_recv()

        found = jnp.where(rep == 2, extra[...], slices[...])
        picks[2][:BLOCK, :] = pick(block_mask(jnp.where(rep == 2, index_of(0), index_of(1))), split(found))
        index = jnp.concatenate([index_of(s) for s in range(2, BLOCKS)], axis=1)
        picks[2][BLOCK:, :] = pick(block_mask(index), split(slices[...]))

    def pair(s):
        half, chunk = COUNTS[s] // 2, COUNTS[s] // 2 // SIDE
        src = picks[s].at[pl.ds((1 - core) * half, half), :]
        flying["pair", s] = send(src, pairs[s], pair_sems, (s,), (partner, rep))

    def first(s):
        half, chunk = COUNTS[s] // 2, COUNTS[s] // 2 // SIDE
        flying["pair", s].wait()
        halves[s][...] = picks[s][pl.ds(core * half, half), :] + pairs[s][...]
        flying["first", s] = []
        for d in ORDER:
            peer, place = first_peer(d)
            src = halves[s].at[pl.ds(place * chunk, chunk), :]
            flying["first", s].append(send(src, firsts[s].at[d - 1], axis_sems, (s, 0, d - 1), (peer, rep)))

    def second(s):
        half, chunk = COUNTS[s] // 2, COUNTS[s] // 2 // SIDE
        total = halves[s][pl.ds(spot * chunk, chunk), :]
        for copy in flying["first", s]:
            copy.wait()
        for d in range(1, SIDE):
            total = total + firsts[s][d - 1]
        owns[s][0] = total
        flying["second", s] = []
        for d in ORDER:
            where = (second_peer(d), rep)
            flying["second", s].append(send(owns[s].at[0], seconds[s].at[d - 1], axis_sems, (s, 1, d - 1), where))

    def gather(s):
        half, chunk = COUNTS[s] // 2, COUNTS[s] // 2 // SIDE
        for copy in flying["second", s]:
            copy.wait()
        total = owns[s][0]
        for d in range(1, SIDE):
            total = total + seconds[s][d - 1]
        owns[s][1] = total
        place = pl.ds(core * half + spot * chunk, chunk)
        fulls[s][place, :] = total
        flying["gather", s] = {}
        for d in ORDER:
            where = (first_peer(d)[0], rep)
            flying["gather", s][d] = send(owns[s].at[1], fulls[s].at[place, :], axis_sems, (s, 2, d - 1), where)
        flying["gather", s][0] = send(owns[s].at[1], fulls[s].at[place, :], fwd_sems, (s, 0), (partner, rep))

    def forward(s):
        half, chunk = COUNTS[s] // 2, COUNTS[s] // 2 // SIDE
        flying["forward", s] = []
        for d in (1, 7, 2, 6, 3, 5, 4):
            flying["gather", s][d].wait()
            source = lax.rem(spot + SIDE - d, SIDE)
            place = pl.ds(core * half + source * chunk, chunk)
            here = fulls[s].at[place, :]
            flying["forward", s].append(send(here, here, fwd_sems, (s, d), (partner, rep)))

    def landed(s):
        flying["gather", s][0].wait()
        for copy in flying["forward", s]:
            copy.wait()
        if s < 2:
            where = slice(0, BLOCK) if s == 0 else slice(BLOCK, BLOCKS * BLOCK)
            for n, part in enumerate(split(fulls[s][:, :EARLY])):
                parts[n, where, :] = part

    def products(left, left_rows, right_rows, terms):
        total = None
        for a, b in terms:
            term = lax.dot_general(
                left[a, left_rows, :], parts[b, right_rows, :], (((1,), (1,)), ((), ())),
                preferred_element_type=jnp.float32,
            )
            total = term if total is None else total + term
        return total

    def slot(s):
        return fulls[0][:, EARLY:] if s == 0 else fulls[2][(s - 1) * BLOCK:s * BLOCK, :]

    def weighed(place, value):
        return jnp.where(rep == place, value, 0.0)

    def column_part(s, t):
        value = slot(s)
        if s == 0:
            return value
        if t == s:
            return weighed(t, 0.5 * (value + value.T))
        if s == 1:
            return 0.5 * (weighed(0, value) + weighed(2, value.T))
        if (s, t) == (3, 2):
            return 0.5 * (weighed(2, value) + weighed(3, slot(2).T))
        return weighed(t, value)

    def gsum(s):
        terms = ((1, 1), (0, 2), (2, 0), (0, 1), (1, 0), (0, 0))
        gram = products(parts, block_cols(s), slice(0, s * BLOCK + BLOCK), terms)
        for t in range(s + 1):
            gparts[s][:, block_cols(t)] = column_part(s, t) - gram[:, block_cols(t)]
        mine = pl.ds(core * HALF, HALF)
        flying["gsum", s] = send(gparts[s].at[mine, :], gxs[s].at[0], gx_sems, (s, 0), (rows, near))

    def gnext(s):
        flying["gsum", s].wait()
        gaccs[s][...] = gparts[s][pl.ds(core * HALF, HALF), :] + gxs[s][0]
        flying["gnext", s] = send(gaccs[s].at[:, :], gxs[s].at[1], gx_sems, (s, 1), (rows, next_near))

    def gpair(s):
        mine = pl.ds(core * HALF, HALF)
        flying["gnext", s].wait()
        gsums[s][mine, :] = gaccs[s][...] + gxs[s][1]
        flying["gpair", s] = send(gsums[s].at[mine, :], gsums[s].at[mine, :], gpair_sems, (s,), (partner, rep))

    def rows_of(place):
        return pl.ds(place * own_rows, own_rows)

    def multiply(n):
        where = slice(0, BLOCK) if n == 0 else slice(BLOCK, BLOCKS * BLOCK)
        partials[n][...] = products(prev_parts, slice(None), where, ((0, 1), (1, 0), (0, 0)))

    def scatter(n):
        flying["scatter", n] = [
            send(partials[n].at[rows_of(place), :], rress[n].at[slot_of], res_sems, (n, slot_of), (rows, near))
            for slot_of, place in ((1, opposite), (0, near))
        ]

    def scatter_next(n):
        for copy in flying["scatter", n]:
            copy.wait()
        raccs[n][...] = partials[n][rows_of(next_near), :] + rress[n][1]
        flying["scatter_next", n] = send(raccs[n].at[:, :], rress[n].at[2], res_sems, (n, 2), (rows, next_near))

    def collect(n):
        flying["scatter_next", n].wait()
        total = (partials[n][rows_of(rep), :] + rress[n][0]) + rress[n][2]
        lanes = slice(0, BLOCK) if n == 0 else slice(BLOCK, BLOCKS * BLOCK)
        vectors_ref[:, lanes] = columns_ref[:, lanes] - total

    def update(t):
        below = lower[t + 1:, :, block_cols(t)].reshape((BLOCKS - 1 - t) * BLOCK, BLOCK)
        lanes = slice((t + 1) * BLOCK, BLOCKS * BLOCK)
        vectors_ref[:, lanes] = vectors_ref[:, lanes] - dot_nt(vectors_ref[:, block_cols(t)], below)

    def solve(s):
        vectors_ref[:, block_cols(s)] = dot_nt(vectors_ref[:, block_cols(s)], inverse[s])

    def prepare(s, t):
        row = dot_nt(gsums[s][:, block_cols(t)], inverse[t])
        lower[s, :, block_cols(t)] = row
        below = lower[t + 1:s + 1, :, block_cols(t)].reshape((s - t) * BLOCK, BLOCK)
        lanes = slice((t + 1) * BLOCK, (s + 1) * BLOCK)
        gsums[s][:, lanes] = gsums[s][:, lanes] - dot_nt(row, below)

    def squares():
        total = None
        for s in range(BLOCKS):
            vec = vectors_ref[:, block_cols(s)]
            total = vec * vec if total is None else total + vec * vec
        ones = jnp.ones((8, BLOCK), jnp.float32)
        diag_ref[...] = diagonal_ref[...] - dot_nt(ones, total)[0:1, :]

    def arrive(s):
        flying["gpair", s].wait()

    def factor(s, gaps):
        for k in range(BLOCK // BASE):
            here = slice(k * BASE, k * BASE + BASE)
            lane = lax.broadcasted_iota(jnp.int32, (BASE, BLOCK), 1)
            sub = lax.broadcasted_iota(jnp.int32, (BASE, BLOCK), 0)
            eye = jnp.where(lane == sub + k * BASE, 1.0, 0.0)
            wide = jnp.concatenate([gsums[s][here, block_cols(s)], eye], axis=1)
            if k:
                done = slice(0, k * BASE)
                wide = wide - dot_tn(upper[done, here], upper[done, :])
            for step in gaps.get(k, ()):
                step()
            upper[here, :] = eliminate(wide[:, here], wide)
        inverse[s] = upper[:, BLOCK:]

    def later(work, *which):
        return lambda: work(*which)

    pick_first()
    pick_rest_early()
    pl.semaphore_wait(barrier, 2 * (SIDE - 1) + REPS)
    pair(0)
    pair(1)
    swap()
    first(0)
    first(1)
    pick_rest_late()
    pair(2)
    second(0)
    first(2)
    second(1)
    gather(0)
    second(2)
    forward(0)
    landed(0)
    gsum(0)
    gather(1)
    gather(2)
    gnext(0)
    multiply(0)
    gpair(0)
    scatter(0)
    arrive(0)
    forward(1)
    forward(2)
    landed(1)
    landed(2)
    gsum(1)
    gsum(2)
    gsum(3)
    scatter_next(0)
    factor(0, {})
    gnext(1)
    gnext(2)
    gnext(3)
    gpair(1)
    multiply(1)
    scatter(1)
    collect(0)
    solve(0)
    arrive(1)
    prepare(1, 0)
    factor(1, {
        0: (later(gpair, 2),),
        1: (later(gpair, 3),),
        2: (later(arrive, 2), later(prepare, 2, 0)),
    })
    prepare(2, 1)
    factor(2, {
        0: (later(scatter_next, 1), later(arrive, 3), later(prepare, 3, 0)),
        1: (later(prepare, 3, 1),),
    })
    prepare(3, 2)
    factor(3, {
        0: (later(collect, 1), later(update, 0)),
        1: (later(solve, 1), later(update, 1)),
        2: (later(solve, 2),),
        3: (later(update, 2),),
    })
    solve(3)
    squares()


def per_device(pivots, previous, columns, diagonal):
    f32 = jnp.float32
    own_rows = columns.shape[0]
    block_rows = previous.shape[0]
    vmem = lambda *shape: pltpu.VMEM(shape, f32)
    each = lambda build: [build(s) for s in range(BLOCKS)]
    scratch = []
    for build in (
        lambda n, w: vmem(n, w), lambda n, w: vmem(n // 2, w), lambda n, w: vmem(n // 2, w),
        lambda n, w: vmem(SIDE - 1, n // 2 // SIDE, w), lambda n, w: vmem(2, n // 2 // SIDE, w),
        lambda n, w: vmem(SIDE - 1, n // 2 // SIDE, w), lambda n, w: vmem(n, w),
    ):
        scratch += [build(n, w) for n, w in zip(COUNTS, LANES)]
    scratch += each(lambda s: vmem(BLOCK, BLOCK * (s + 1)))
    scratch += each(lambda s: vmem(2, HALF, BLOCK * (s + 1)))
    scratch += each(lambda s: vmem(HALF, BLOCK * (s + 1)))
    scratch += each(lambda s: vmem(BLOCK, BLOCK * (s + 1)))
    scratch += [vmem(block_rows, n) for n in COUNTS[:2]]
    scratch += [vmem(REPS - 1, own_rows, n) for n in COUNTS[:2]]
    scratch += [vmem(own_rows, n) for n in COUNTS[:2]]
    scratch += [
        pltpu.VMEM((3, block_rows, EARLY), jnp.bfloat16), vmem(block_rows, BLOCK), vmem(block_rows, BLOCK),
        vmem(BLOCK, 2 * BLOCK), vmem(BLOCKS, BLOCK, BLOCKS * BLOCK), vmem(BLOCKS, BLOCK, BLOCK),
        pltpu.VMEM((3, BLOCKS * BLOCK, EARLY), jnp.bfloat16),
    ]
    dma = pltpu.SemaphoreType.DMA
    scratch += [
        dma((2, 2 * (REPS - 1))), dma((2, 3)), dma((2, 3, 3, SIDE - 1)), dma((2, 3, SIDE)),
        dma((2, BLOCKS, 2)), dma((2, BLOCKS)), dma((2, 2, REPS - 1)),
    ]
    space = pl.BlockSpec(memory_space=pltpu.VMEM)
    vectors, diag = pl.pallas_call(
        kernel,
        out_shape=(jax.ShapeDtypeStruct(columns.shape, f32), jax.ShapeDtypeStruct((1, own_rows), f32)),
        in_specs=[space] * 4,
        out_specs=[space] * 2,
        scratch_shapes=scratch,
        compiler_params=pltpu.CompilerParams(collective_id=0, has_side_effects=True),
    )(pivots, previous, columns, diagonal.reshape(1, own_rows))
    return vectors, diag.reshape(own_rows)


def solution(mesh):
    placed = (P(), P("rows", "rep"), P(("rows", "rep"), None), P(("rows", "rep")))
    return jax.shard_map(
        per_device,
        mesh=mesh,
        in_specs=placed,
        out_specs=(P(("rows", "rep"), None), P(("rows", "rep"))),
        check_vma=False,
    )
```

```python
import functools

import jax
import jax.numpy as jnp
from jax import lax
from jax.experimental import pallas as pl
from jax.experimental.pallas import tpu as pltpu
from jax.sharding import PartitionSpec as P

HIGHEST = lax.Precision.HIGHEST
MESH = pl.DeviceIdType.MESH
BLOCK = 128
BLOCKS = 4
HALF = BLOCK // 2
EARLY = 384
SIDE = 8
REPS = 4
COUNTS = (BLOCK, (BLOCKS - 1) * BLOCK, (BLOCKS - 1) * BLOCK)
LANES = (EARLY + BLOCK, EARLY, BLOCK)
ORDER = (4, 3, 5, 2, 6, 1, 7)
BASE = 32
TILES = BASE // 8


def dot_tn(left, right):
    return lax.dot_general(
        left, right, (((0,), (0,)), ((), ())), precision=HIGHEST, preferred_element_type=jnp.float32
    )


def spread(tile, row):
    return jnp.broadcast_to(tile[row:row + 1, :], tile.shape)


def eliminate(square, wide):
    sub = lax.broadcasted_iota(jnp.int32, (8, 128), 0)
    cols = []
    for k in range(BASE):
        cols.append([None] * TILES)
        for v in range(k // 8, TILES):
            cols[k][v] = jnp.broadcast_to(square[8 * v:8 * v + 8, k:k + 1], (8, 128))
    lanes = wide.shape[1] // 128
    work = [[wide[8 * v:8 * v + 8, 128 * l:128 * l + 128] for l in range(lanes)] for v in range(TILES)]
    pivots = []
    for j in range(BASE):
        top, row = j // 8, j % 8
        pivot = spread(cols[j][top], row)
        pivots.append(pivot)
        inverse = 1.0 / pivot
        factor = [None] * TILES
        for v in range(top, TILES):
            value = cols[j][v] * inverse
            factor[v] = jnp.where(sub > row, value, 0.0) if v == top else value
        for k in range(j + 1, BASE):
            value = spread(cols[j][k // 8], k % 8)
            for v in range(k // 8, TILES):
                cols[k][v] = cols[k][v] - factor[v] * value
        for l in range(lanes):
            value = spread(work[top][l], row)
            for v in range(top, TILES):
                work[v][l] = work[v][l] - factor[v] * value
    out = []
    for v in range(TILES):
        pivot = pivots[8 * v]
        for s in range(1, 8):
            pivot = jnp.where(sub == s, pivots[8 * v + s], pivot)
        scale = lax.rsqrt(pivot)
        scale = scale * (1.5 - 0.5 * pivot * scale * scale)
        out.append(jnp.concatenate([work[v][l] * scale for l in range(lanes)], axis=1))
    return jnp.concatenate(out, axis=0)


def dot_nt(left, right, precision=HIGHEST):
    return lax.dot_general(
        left, right, (((1,), (1,)), ((), ())), precision=precision, preferred_element_type=jnp.float32
    )


def split(values):
    parts = []
    for _ in range(3):
        part = values.astype(jnp.bfloat16)
        values = values - part.astype(jnp.float32)
        parts.append(part)
    return parts


def dot_parts(left, right):
    a, b = split(left), split(right)
    terms = [dot_nt(a[m], b[n], None) for m, n in ((0, 1), (1, 0), (0, 0))]
    return (terms[0] + terms[1]) + terms[2]


def pick(mask, parts):
    total = None
    for part in parts:
        term = lax.dot_general(mask, part, (((0,), (0,)), ((), ())), preferred_element_type=jnp.float32)
        total = term if total is None else total + term
    return total


def block_cols(s):
    return slice(s * BLOCK, s * BLOCK + BLOCK)


def kernel(pivots_ref, previous_ref, columns_ref, diagonal_ref, vectors_ref, diag_ref, *scratch):
    picks, pairs, halves, firsts, owns, seconds, fulls = (scratch[3 * n:3 * n + 3] for n in range(7))
    scratch = scratch[21:]
    gparts, gxs, gaccs, gsums = (scratch[BLOCKS * n:BLOCKS * n + BLOCKS] for n in range(4))
    scratch = scratch[4 * BLOCKS:]
    partials, rress, raccs = scratch[:2], scratch[2:4], scratch[4:6]
    prev_parts, slices, extra, upper, lower, inverse, parts = scratch[6:13]
    swap_sems, pair_sems, axis_sems, fwd_sems, gx_sems, gpair_sems, res_sems = scratch[13:]
    rows = lax.axis_index("rows")
    rep = lax.axis_index("rep")
    core = lax.rem(rows, 2)
    chip_z = lax.rem(rows // 2, SIDE)
    chip_y = rows // (2 * SIDE)
    spot = (1 - core) * chip_y + core * chip_z
    block_rows = previous_ref.shape[0]
    own_rows = columns_ref.shape[0]

    def at(y, z, c):
        return (y * SIDE + z) * 2 + c

    def first_peer(d):
        y = lax.rem(chip_y + (1 - core) * d, SIDE)
        z = lax.rem(chip_z + core * d, SIDE)
        return at(y, z, core), lax.rem(spot + d, SIDE)

    def second_peer(d):
        y = lax.rem(chip_y + core * d, SIDE)
        z = lax.rem(chip_z + (1 - core) * d, SIDE)
        return at(y, z, core)

    partner = at(chip_y, chip_z, 1 - core)
    turn = (1 - 2 * lax.rem(rep, 2)) * (1 - 2 * core)
    near = lax.rem(rep + turn + REPS, REPS)
    next_near = lax.rem(rep - turn + REPS, REPS)
    opposite = lax.rem(rep + 2, REPS)
    barrier = pltpu.get_barrier_semaphore()
    for d in range(1, SIDE):
        pl.semaphore_signal(barrier, inc=1, device_id=(first_peer(d)[0], rep), device_id_type=MESH)
        pl.semaphore_signal(barrier, inc=1, device_id=(second_peer(d), rep), device_id_type=MESH)
    for d in range(1, REPS):
        pl.semaphore_signal(barrier, inc=1, device_id=(rows, lax.rem(rep + d, REPS)), device_id_type=MESH)
    pl.semaphore_signal(barrier, inc=1, device_id=(partner, rep), device_id_type=MESH)

    def send(src, dst, sems, slot, where):
        copy = pltpu.make_async_remote_copy(
            src_ref=src, dst_ref=dst, send_sem=sems.at[(0,) + slot], recv_sem=sems.at[(1,) + slot],
            device_id=where, device_id_type=MESH,
        )
        copy.start()
        return copy

    flying = {}

    def index_of(s):
        return pivots_ref[s // 2:s // 2 + 1, block_cols(s % 2)]

    def block_mask(index):
        place = lax.broadcasted_iota(jnp.int32, (block_rows, index.shape[1]), 0) + rows * block_rows
        return jnp.where(place == index, 1.0, 0.0).astype(jnp.bfloat16)

    def pick_first():
        for n, part in enumerate(split(previous_ref[...])):
            prev_parts[n] = part
        picks[0][:, :EARLY] = pick(block_mask(index_of(0)), [prev_parts[n] for n in range(3)])
        place = lax.broadcasted_iota(jnp.int32, (BLOCK, BLOCK), 0)
        own = place + (rows * REPS + rep) * own_rows
        mask = jnp.where((own == index_of(0)) & (place < own_rows), 1.0, 0.0).astype(jnp.bfloat16)
        pad = jnp.zeros((BLOCK - own_rows, BLOCK), jnp.float32)
        found = pick(mask, split(jnp.concatenate([columns_ref[:, :BLOCK], pad], axis=0)))
        picks[0][:, EARLY:] = 0.5 * (found + found.T)

    def swap():
        flying["swap"] = []
        here = pl.ds(rep * own_rows, own_rows)
        for d in (2, 1, 3):
            other = lax.rem(rep + d, REPS)
            src = columns_ref.at[:, pl.ds(pl.multiple_of(other * BLOCK, BLOCK), BLOCK)]
            flying["swap"].append(send(src, slices.at[here, :], swap_sems, (d - 1,), (rows, other)))
        slices[here, :] = columns_ref[:, pl.ds(pl.multiple_of(rep * BLOCK, BLOCK), BLOCK)]
        extra[here, :] = columns_ref[:, block_cols(1)]
        for d in (2, 1, 3):
            other = lax.rem(rep + d, REPS)

            @pl.when(other == 2)
            def _():
                send(columns_ref.at[:, block_cols(1)], extra.at[here, :], swap_sems, (d + 2,), (rows, other)).wait_send()

    def pick_rest_early():
        index = jnp.concatenate([index_of(s) for s in range(1, BLOCKS)], axis=1)
        picks[1][...] = pick(block_mask(index), [prev_parts[n] for n in range(3)])

    def pick_rest_late():
        for copy in flying["swap"]:
            copy.wait()

        @pl.when(rep == 2)
        def _():
            here = pl.ds(rep * own_rows, own_rows)
            for d in (2, 1, 3):
                pltpu.make_async_remote_copy(
                    src_ref=columns_ref.at[:, block_cols(1)], dst_ref=extra.at[here, :], send_sem=swap_sems.at[0, d + 2],
                    recv_sem=swap_sems.at[1, d + 2], device_id=(rows, lax.rem(rep + d, REPS)), device_id_type=MESH,
                ).wait_recv()

        found = jnp.where(rep == 2, extra[...], slices[...])
        picks[2][:BLOCK, :] = pick(block_mask(jnp.where(rep == 2, index_of(0), index_of(1))), split(found))
        index = jnp.concatenate([index_of(s) for s in range(2, BLOCKS)], axis=1)
        picks[2][BLOCK:, :] = pick(block_mask(index), split(slices[...]))

    def pair(s):
        half, chunk = COUNTS[s] // 2, COUNTS[s] // 2 // SIDE
        src = picks[s].at[pl.ds((1 - core) * half, half), :]
        flying["pair", s] = send(src, pairs[s], pair_sems, (s,), (partner, rep))

    def first(s):
        half, chunk = COUNTS[s] // 2, COUNTS[s] // 2 // SIDE
        flying["pair", s].wait()
        halves[s][...] = picks[s][pl.ds(core * half, half), :] + pairs[s][...]
        flying["first", s] = []
        for d in ORDER:
            peer, place = first_peer(d)
            src = halves[s].at[pl.ds(place * chunk, chunk), :]
            flying["first", s].append(send(src, firsts[s].at[d - 1], axis_sems, (s, 0, d - 1), (peer, rep)))

    def second(s):
        half, chunk = COUNTS[s] // 2, COUNTS[s] // 2 // SIDE
        total = halves[s][pl.ds(spot * chunk, chunk), :]
        for copy in flying["first", s]:
            copy.wait()
        for d in range(1, SIDE):
            total = total + firsts[s][d - 1]
        owns[s][0] = total
        flying["second", s] = []
        for d in ORDER:
            where = (second_peer(d), rep)
            flying["second", s].append(send(owns[s].at[0], seconds[s].at[d - 1], axis_sems, (s, 1, d - 1), where))

    def gather(s):
        half, chunk = COUNTS[s] // 2, COUNTS[s] // 2 // SIDE
        for copy in flying["second", s]:
            copy.wait()
        total = owns[s][0]
        for d in range(1, SIDE):
            total = total + seconds[s][d - 1]
        owns[s][1] = total
        place = pl.ds(core * half + spot * chunk, chunk)
        fulls[s][place, :] = total
        flying["gather", s] = {}
        for d in ORDER:
            where = (first_peer(d)[0], rep)
            flying["gather", s][d] = send(owns[s].at[1], fulls[s].at[place, :], axis_sems, (s, 2, d - 1), where)
        flying["gather", s][0] = send(owns[s].at[1], fulls[s].at[place, :], fwd_sems, (s, 0), (partner, rep))

    def forward(s):
        half, chunk = COUNTS[s] // 2, COUNTS[s] // 2 // SIDE
        flying["forward", s] = []
        for d in (1, 7, 2, 6, 3, 5, 4):
            flying["gather", s][d].wait()
            source = lax.rem(spot + SIDE - d, SIDE)
            place = pl.ds(core * half + source * chunk, chunk)
            here = fulls[s].at[place, :]
            flying["forward", s].append(send(here, here, fwd_sems, (s, d), (partner, rep)))

    def landed(s):
        flying["gather", s][0].wait()
        for copy in flying["forward", s]:
            copy.wait()
        if s < 2:
            where = slice(0, BLOCK) if s == 0 else slice(BLOCK, BLOCKS * BLOCK)
            for n, part in enumerate(split(fulls[s][:, :EARLY])):
                parts[n, where, :] = part

    def products(left, left_rows, right_rows, terms):
        total = None
        for a, b in terms:
            term = lax.dot_general(
                left[a, left_rows, :], parts[b, right_rows, :], (((1,), (1,)), ((), ())),
                preferred_element_type=jnp.float32,
            )
            total = term if total is None else total + term
        return total

    def slot(s):
        return fulls[0][:, EARLY:] if s == 0 else fulls[2][(s - 1) * BLOCK:s * BLOCK, :]

    def weighed(place, value):
        return jnp.where(rep == place, value, 0.0)

    def column_part(s, t):
        value = slot(s)
        if s == 0:
            return value
        if t == s:
            return weighed(t, 0.5 * (value + value.T))
        if s == 1:
            return 0.5 * (weighed(0, value) + weighed(2, value.T))
        if (s, t) == (3, 2):
            return 0.5 * (weighed(2, value) + weighed(3, slot(2).T))
        return weighed(t, value)

    def gsum(s):
        terms = ((1, 1), (0, 2), (2, 0), (0, 1), (1, 0), (0, 0))
        gram = products(parts, block_cols(s), slice(0, s * BLOCK + BLOCK), terms)
        for t in range(s + 1):
            gparts[s][:, block_cols(t)] = column_part(s, t) - gram[:, block_cols(t)]
        mine = pl.ds(core * HALF, HALF)
        flying["gsum", s] = send(gparts[s].at[mine, :], gxs[s].at[0], gx_sems, (s, 0), (rows, near))

    def gnext(s):
        flying["gsum", s].wait()
        gaccs[s][...] = gparts[s][pl.ds(core * HALF, HALF), :] + gxs[s][0]
        flying["gnext", s] = send(gaccs[s].at[:, :], gxs[s].at[1], gx_sems, (s, 1), (rows, next_near))

    def gpair(s):
        mine = pl.ds(core * HALF, HALF)
        flying["gnext", s].wait()
        gsums[s][mine, :] = gaccs[s][...] + gxs[s][1]
        flying["gpair", s] = send(gsums[s].at[mine, :], gsums[s].at[mine, :], gpair_sems, (s,), (partner, rep))

    def rows_of(place):
        return pl.ds(place * own_rows, own_rows)

    def multiply(n):
        where = slice(0, BLOCK) if n == 0 else slice(BLOCK, BLOCKS * BLOCK)
        partials[n][...] = products(prev_parts, slice(None), where, ((0, 1), (1, 0), (0, 0)))

    def scatter(n):
        flying["scatter", n] = [
            send(partials[n].at[rows_of(place), :], rress[n].at[slot_of], res_sems, (n, slot_of), (rows, near))
            for slot_of, place in ((1, opposite), (0, near))
        ]

    def scatter_next(n):
        for copy in flying["scatter", n]:
            copy.wait()
        raccs[n][...] = partials[n][rows_of(next_near), :] + rress[n][1]
        flying["scatter_next", n] = send(raccs[n].at[:, :], rress[n].at[2], res_sems, (n, 2), (rows, next_near))

    def collect(n):
        flying["scatter_next", n].wait()
        total = (partials[n][rows_of(rep), :] + rress[n][0]) + rress[n][2]
        lanes = slice(0, BLOCK) if n == 0 else slice(BLOCK, BLOCKS * BLOCK)
        vectors_ref[:, lanes] = columns_ref[:, lanes] - total

    def update(t):
        below = lower[t + 1:, :, block_cols(t)].reshape((BLOCKS - 1 - t) * BLOCK, BLOCK)
        lanes = slice((t + 1) * BLOCK, BLOCKS * BLOCK)
        vectors_ref[:, lanes] = vectors_ref[:, lanes] - dot_parts(vectors_ref[:, block_cols(t)], below)

    def solve(s):
        vectors_ref[:, block_cols(s)] = dot_parts(vectors_ref[:, block_cols(s)], inverse[s])

    def prepare(s, t):
        row = dot_nt(gsums[s][:, block_cols(t)], inverse[t])
        lower[s, :, block_cols(t)] = row
        below = lower[t + 1:s + 1, :, block_cols(t)].reshape((s - t) * BLOCK, BLOCK)
        lanes = slice((t + 1) * BLOCK, (s + 1) * BLOCK)
        gsums[s][:, lanes] = gsums[s][:, lanes] - dot_nt(row, below)

    def squares():
        total = None
        for s in range(BLOCKS):
            vec = vectors_ref[:, block_cols(s)]
            total = vec * vec if total is None else total + vec * vec
        ones = jnp.ones((8, BLOCK), jnp.bfloat16)
        sums = [dot_nt(ones, part, None) for part in split(total)]
        diag_ref[...] = diagonal_ref[...] - ((sums[2] + sums[1]) + sums[0])[0:1, :]

    def arrive(s):
        flying["gpair", s].wait()

    def factor(s, gaps):
        for k in range(BLOCK // BASE):
            here = slice(k * BASE, k * BASE + BASE)
            lane = lax.broadcasted_iota(jnp.int32, (BASE, BLOCK), 1)
            sub = lax.broadcasted_iota(jnp.int32, (BASE, BLOCK), 0)
            eye = jnp.where(lane == sub + k * BASE, 1.0, 0.0)
            wide = jnp.concatenate([gsums[s][here, block_cols(s)], eye], axis=1)
            if k:
                done = slice(0, k * BASE)
                wide = wide - dot_tn(upper[done, here], upper[done, :])
            for step in gaps.get(k, ()):
                step()
            upper[here, :] = eliminate(wide[:, here], wide)
        inverse[s] = upper[:, BLOCK:]

    def later(work, *which):
        return lambda: work(*which)

    pick_first()
    pick_rest_early()
    pl.semaphore_wait(barrier, 2 * (SIDE - 1) + REPS)
    pair(0)
    pair(1)
    swap()
    first(0)
    first(1)
    pick_rest_late()
    pair(2)
    second(0)
    first(2)
    second(1)
    gather(0)
    second(2)
    forward(0)
    landed(0)
    gsum(0)
    gather(1)
    gather(2)
    gnext(0)
    multiply(0)
    gpair(0)
    scatter(0)
    arrive(0)
    forward(1)
    forward(2)
    landed(1)
    landed(2)
    gsum(1)
    gsum(2)
    gsum(3)
    scatter_next(0)
    factor(0, {})
    gnext(1)
    gnext(2)
    gnext(3)
    gpair(1)
    multiply(1)
    scatter(1)
    collect(0)
    solve(0)
    arrive(1)
    prepare(1, 0)
    factor(1, {
        0: (later(gpair, 2),),
        1: (later(gpair, 3),),
        2: (later(arrive, 2), later(prepare, 2, 0)),
    })
    prepare(2, 1)
    factor(2, {
        0: (later(scatter_next, 1), later(arrive, 3), later(prepare, 3, 0)),
        1: (later(prepare, 3, 1),),
    })
    prepare(3, 2)
    factor(3, {
        0: (later(collect, 1), later(update, 0)),
        1: (later(solve, 1), later(update, 1)),
        2: (later(solve, 2),),
        3: (later(update, 2),),
    })
    solve(3)
    squares()


def per_device(pivots, previous, columns, diagonal):
    f32 = jnp.float32
    own_rows = columns.shape[0]
    block_rows = previous.shape[0]
    vmem = lambda *shape: pltpu.VMEM(shape, f32)
    each = lambda build: [build(s) for s in range(BLOCKS)]
    scratch = []
    for build in (
        lambda n, w: vmem(n, w), lambda n, w: vmem(n // 2, w), lambda n, w: vmem(n // 2, w),
        lambda n, w: vmem(SIDE - 1, n // 2 // SIDE, w), lambda n, w: vmem(2, n // 2 // SIDE, w),
        lambda n, w: vmem(SIDE - 1, n // 2 // SIDE, w), lambda n, w: vmem(n, w),
    ):
        scratch += [build(n, w) for n, w in zip(COUNTS, LANES)]
    scratch += each(lambda s: vmem(BLOCK, BLOCK * (s + 1)))
    scratch += each(lambda s: vmem(2, HALF, BLOCK * (s + 1)))
    scratch += each(lambda s: vmem(HALF, BLOCK * (s + 1)))
    scratch += each(lambda s: vmem(BLOCK, BLOCK * (s + 1)))
    scratch += [vmem(block_rows, n) for n in COUNTS[:2]]
    scratch += [vmem(REPS - 1, own_rows, n) for n in COUNTS[:2]]
    scratch += [vmem(own_rows, n) for n in COUNTS[:2]]
    scratch += [
        pltpu.VMEM((3, block_rows, EARLY), jnp.bfloat16), vmem(block_rows, BLOCK), vmem(block_rows, BLOCK),
        vmem(BLOCK, 2 * BLOCK), vmem(BLOCKS, BLOCK, BLOCKS * BLOCK), vmem(BLOCKS, BLOCK, BLOCK),
        pltpu.VMEM((3, BLOCKS * BLOCK, EARLY), jnp.bfloat16),
    ]
    dma = pltpu.SemaphoreType.DMA
    scratch += [
        dma((2, 2 * (REPS - 1))), dma((2, 3)), dma((2, 3, 3, SIDE - 1)), dma((2, 3, SIDE)),
        dma((2, BLOCKS, 2)), dma((2, BLOCKS)), dma((2, 2, REPS - 1)),
    ]
    space = pl.BlockSpec(memory_space=pltpu.VMEM)
    vectors, diag = pl.pallas_call(
        kernel,
        out_shape=(jax.ShapeDtypeStruct(columns.shape, f32), jax.ShapeDtypeStruct((1, own_rows), f32)),
        in_specs=[space] * 4,
        out_specs=[space] * 2,
        scratch_shapes=scratch,
        compiler_params=pltpu.CompilerParams(collective_id=0, has_side_effects=True),
    )(pivots, previous, columns, diagonal.reshape(1, own_rows))
    return vectors, diag.reshape(own_rows)


def solution(mesh):
    placed = (P(), P("rows", "rep"), P(("rows", "rep"), None), P(("rows", "rep")))
    return jax.shard_map(
        per_device,
        mesh=mesh,
        in_specs=placed,
        out_specs=(P(("rows", "rep"), None), P(("rows", "rep"))),
        check_vma=False,
    )
```
